128 devices in a mesh: rows: 16 (over z, y_hi, core), cols: 8 (over x, y_lo).
Axes of the slice: x: 4, y: 4 (y_hi: 2, y_lo: 2; y = y_hi * 2 + y_lo), z: 4, core: 2. Of those that a mesh axis runs over, the one named last changes fastest.
Arguments:
- feat_query: bfloat16 [256, 512, 2048], P('rows', 'cols'), may hold values from -30 to 30
- feat_key: bfloat16 [256, 512, 2048], P('rows', 'cols'), may hold values from -30 to 30
- w_hidden: bfloat16 [2048, 2048], replicated, may hold values from -0.125 to 0.125
- w_out: bfloat16 [2048, 256], replicated, may hold values from -0.125 to 0.125
- w_prop: bfloat16 [256, 256], replicated, may hold values from -0.375 to 0.375
- valid_mask: int32 [256, 512], P('rows', 'cols'), may hold values 0 or 1
- neg_shard: int32 [16, 8, 8, 2], P('rows', 'cols'), may hold values from 0 to 15, as said below
- neg_block: int32 [16, 8, 8, 2], P('rows', 'cols'), may hold values from 0 to 7
Outputs:
- loss_map: float32 [256, 512], P('rows', 'cols')
The draws below stay inside these ranges and needn't reach their ends.
Inputs may be any that keep to these rules, and one draw needn't show every extreme that they name: `neg_shard`: among the 16 entries of one tile, no shard number appears more than 2 times, and some shard number appears exactly 2 times.
All inputs are finite; a program needn't handle non-finite values. No bound on the sum of `valid_mask` on one device may be relied on, other than what follows from the above.
Results may differ from the reference program's by a relative error of at most 0.0006.
Values may be sent and summed in bfloat16 or wider, within the bound.
No kernel may reach another device: no remote copies, remote signals or barrier semaphores. Data moves between devices by JAX's collectives and lax.ppermute only.
A program may use at most 128 MiB of HBM per device.

```python
import math
import jax
import jax.numpy as jnp
from jax import lax

C = 2048
HID = 2048
P_SIZE = 256
HD = 16
WD = 64
NPER = 2
NH = 256
NW = 512
QB = 8
CAP = 2
N_ROWS = 16
N_COLS = 8


def scene(key):
    base_key = jax.random.fold_in(key, 11)
    common = jax.random.normal(jax.random.fold_in(base_key, 1), (C,), jnp.float32)
    patch_rows = NH // 8
    patch_cols = NW // 8
    strength = jnp.exp(jax.random.uniform(jax.random.fold_in(base_key, 2), (patch_rows, patch_cols), jnp.float32, math.log(0.2), math.log(5.0)))
    region = jax.random.normal(jax.random.fold_in(base_key, 3), (patch_rows, patch_cols, C), jnp.float32)
    field_map = common[None, None, :] + strength[..., None] * region
    return jnp.repeat(jnp.repeat(field_map, 8, axis=0), 8, axis=1)


def jitter_of(key):
    return jax.random.normal(key, (NH, NW, C), jnp.float32)


def draw_feat_query(key, part):
    values = scene(key) + jitter_of(jax.random.fold_in(key, 21))
    return jnp.clip(values, -30.0, 30.0).astype(jnp.bfloat16)


def draw_feat_key(key, part):
    values = scene(key)[:, ::-1] + jitter_of(jax.random.fold_in(key, 22))
    return jnp.clip(values, -30.0, 30.0).astype(jnp.bfloat16)


def requests_of(key):
    base_key = jax.random.fold_in(key, 31)
    slots_total = N_ROWS * CAP
    wanted_count = QB * NPER

    def for_device(device_key):
        shuffled = jax.random.permutation(jax.random.fold_in(device_key, 1), slots_total)
        position = jnp.argsort(shuffled).astype(jnp.int32)
        candidate = jnp.arange(slots_total, dtype=jnp.int32)
        leading = shuffled[0] // CAP
        scores = jnp.where(candidate // CAP == leading, candidate % CAP - CAP, position)
        chosen = jnp.argsort(scores)[:wanted_count].astype(jnp.int32)
        shard_ids = chosen // CAP
        reorder = jax.random.permutation(jax.random.fold_in(device_key, 2), wanted_count)
        shard_ids = shard_ids[reorder]
        block_ids = jax.random.randint(jax.random.fold_in(device_key, 3), (wanted_count,), 0, QB, jnp.int32)
        return (shard_ids, block_ids)
    device_keys = jax.random.split(base_key, N_ROWS * N_COLS)
    shard_ids, block_ids = jax.vmap(for_device)(device_keys)
    return (shard_ids.reshape(N_ROWS, N_COLS, QB, NPER), block_ids.reshape(N_ROWS, N_COLS, QB, NPER))


def draw_neg_shard(key, part):
    return requests_of(key)[0]


def draw_neg_block(key, part):
    return requests_of(key)[1]


def with_ends(values, own_key, low, top_value):
    extent = values.shape
    spot = [jax.random.randint(jax.random.fold_in(own_key, axis), (), 0, extent[axis]) for axis in range(len(extent))]
    values = values.at[tuple(spot)].set(low)
    longest = extent.index(max(extent))
    spot[longest] = (spot[longest] + 1) % extent[longest]
    return values.at[tuple(spot)].set(top_value)


def noise(own_key, dims, deviation, limit, held_as=jnp.bfloat16):
    return jnp.clip(deviation * jax.random.normal(own_key, dims, jnp.float32), -limit, limit).astype(held_as)


def setup_inputs(seed: int = 0) -> dict:
    streams_of = jax.random.split(jax.random.key(seed), 9)
    feat_query = draw_feat_query(jax.random.fold_in(streams_of[8], 71), 0)
    feat_key = draw_feat_key(jax.random.fold_in(streams_of[8], 71), 0)
    w_hidden = noise(streams_of[2], (C, HID), C ** -0.5, 0.125)
    w_out = noise(streams_of[3], (HID, P_SIZE), HID ** -0.5, 0.125)
    w_prop = noise(streams_of[4], (P_SIZE, P_SIZE), P_SIZE ** -0.5, 0.375)
    valid_mask = with_ends((jax.random.randint(streams_of[5], (NH, NW), 0, 8) < 7).astype(jnp.int32), jax.random.fold_in(streams_of[5], 1), 0, 1)
    neg_shard = draw_neg_shard(jax.random.fold_in(streams_of[8], 71), 0)
    neg_block = draw_neg_block(jax.random.fold_in(streams_of[8], 71), 0)
    return dict(feat_query=feat_query, feat_key=feat_key, w_hidden=w_hidden, w_out=w_out, w_prop=w_prop, valid_mask=valid_mask, neg_shard=neg_shard, neg_block=neg_block)


epsilon = 1e-06
sharpness_divisor = 0.1

def normalize(vector):
    return vector * lax.rsqrt(lax.optimization_barrier(jnp.sum(vector * vector, axis=-1, keepdims=True)) + epsilon)

def project(feat_map, w_hidden, w_out):
    rows_all, cols_all, channels = feat_map.shape
    band_stack = feat_map.reshape(N_ROWS, HD * cols_all, channels)

    def one_band(band_rows):
        hidden = jnp.maximum(jnp.dot(band_rows, w_hidden, preferred_element_type=jnp.float32), 0.0).astype(jnp.bfloat16)
        return normalize(jnp.dot(hidden, w_out, preferred_element_type=jnp.float32)).astype(jnp.bfloat16)
    return lax.map(one_band, band_stack).reshape(rows_all, cols_all, -1)

def to_tiles(field_map):
    return field_map.reshape(N_ROWS, HD, N_COLS, WD, -1).transpose(0, 2, 1, 3, 4).reshape(N_ROWS, N_COLS, QB, 128, field_map.shape[-1])

def reference(feat_query, feat_key, w_hidden, w_out, w_prop, valid_mask, neg_shard, neg_block):
    query_map = project(feat_query, w_hidden, w_out)
    target_embedding_lattice = project(feat_key, w_hidden, w_out)
    proj_width = query_map.shape[-1]
    padded = jnp.pad(query_map, ((1, 1), (1, 1), (0, 0)))
    carried = jnp.dot(padded.reshape(-1, proj_width), w_prop, preferred_element_type=jnp.float32).reshape(NH + 2, NW + 2, proj_width)
    centre = query_map.astype(jnp.float32)
    spread = jnp.zeros((NH, NW, proj_width), jnp.float32)
    for row_off in range(3):
        for col_off in range(3):
            beside = padded[row_off:row_off + NH, col_off:col_off + NW].astype(jnp.float32)
            cosine = lax.optimization_barrier(jnp.sum(centre * beside, axis=-1))
            weight = jnp.maximum(cosine, 0.0) ** 2
            spread = spread + weight[..., None] * carried[row_off:row_off + NH, col_off:col_off + NW]
    diffused_pixel_embeddings = normalize(spread).astype(jnp.bfloat16)
    matched_pair_agreement = lax.optimization_barrier(jnp.sum(diffused_pixel_embeddings.astype(jnp.float32) * target_embedding_lattice[:, ::-1].astype(jnp.float32), axis=-1)) / sharpness_divisor
    key_tiles = to_tiles(target_embedding_lattice)
    anchor_patch_lattice = to_tiles(diffused_pixel_embeddings)
    col_ids = jnp.arange(N_COLS, dtype=jnp.int32)[None, :, None, None]
    contrast_pair_agreements = key_tiles[neg_shard, col_ids, neg_block]
    cosine_match_energies = jnp.einsum('irgjp,irgzkp->irgjzk', anchor_patch_lattice.astype(jnp.float32), contrast_pair_agreements.astype(jnp.float32)) / sharpness_divisor
    negsum = lax.optimization_barrier(jnp.sum(jnp.exp(cosine_match_energies), axis=(4, 5)))
    negsum = negsum.reshape(N_ROWS, N_COLS, HD, WD).transpose(0, 2, 1, 3).reshape(NH, NW)
    return valid_mask.astype(jnp.float32) * (jnp.log(jnp.exp(matched_pair_agreement) + negsum) - matched_pair_agreement)
```

```python
import functools

import jax
import jax.numpy as jnp
from jax import lax
from jax.experimental import pallas as pl
from jax.experimental.pallas import tpu as pltpu
from jax.sharding import PartitionSpec as P


epsilon = 1e-06
inverse_divisor = 10.0
CAP = 2
LANES = 128
VMEM = pl.BlockSpec(memory_space=pltpu.VMEM)
SMEM = pl.BlockSpec(memory_space=pltpu.SMEM)
ANY = pl.BlockSpec(memory_space=pl.ANY)
LIMIT = 60 * 2**20
SMALL = pltpu.CompilerParams(vmem_limit_bytes=12 * 2**20)
f32 = jnp.float32
bf16 = jnp.bfloat16


def normalize(vector):
    return vector * lax.rsqrt(jnp.sum(vector * vector, axis=-1, keepdims=True) + epsilon)


def transposed_dot(left, right):
    return lax.dot_general(left, right, (((1,), (1,)), ((), ())), preferred_element_type=f32)


def plan_kernel(shard_ref, block_ref, want_ref, slot_ref):
    _, _, per, blocks = shard_ref.shape
    shards = want_ref.shape[0]
    rows = lax.broadcasted_iota(jnp.int32, (shards, LANES), 0)
    lanes = lax.broadcasted_iota(jnp.int32, (shards, LANES), 1)
    want = jnp.zeros((shards, LANES), jnp.int32)
    chosen = []
    for block in range(blocks):
        for n in range(per):
            shard = shard_ref[0, 0, n, block]
            rank = jnp.int32(0)
            for other in chosen:
                rank = rank + (other == shard).astype(jnp.int32)
            rank = jnp.minimum(rank, CAP - 1)
            chosen.append(shard)
            slot_ref[block * per + n] = shard * CAP + rank
            want = jnp.where((rows == shard) & (lanes == rank), block_ref[0, 0, n, block], want)
    want_ref[...] = want.reshape(want_ref.shape)


def plan_slots(neg_shard, neg_block, shards):
    entries = neg_shard.size
    return pl.pallas_call(
        plan_kernel,
        in_specs=[SMEM, SMEM],
        out_specs=[VMEM, SMEM],
        out_shape=[
            jax.ShapeDtypeStruct((shards, 1, LANES), jnp.int32),
            jax.ShapeDtypeStruct((entries,), jnp.int32),
        ],
        compiler_params=SMALL,
        name="plan_slots",
    )(neg_shard.transpose(0, 1, 3, 2), neg_block.transpose(0, 1, 3, 2))


ROWS = 256
PARTS = 8


def project_kernel(feat_ref, hidden_hbm, out_hbm, map_ref, hidden_w, out_w, sem):
    step = pl.program_id(0)
    span = hidden_w.shape[1] // PARTS

    def piece(index):
        cut = pl.ds(index * span, span)
        return pltpu.make_async_copy(hidden_hbm.at[:, cut], hidden_w.at[:, cut], sem.at[index])

    def tail():
        return pltpu.make_async_copy(out_hbm, out_w, sem.at[PARTS])

    def finish(raw):
        map_ref[...] = normalize(raw).astype(map_ref.dtype)

    def layer(cut):
        hidden = jnp.dot(feat_ref[...], hidden_w[:, cut], preferred_element_type=f32)
        hidden = jnp.maximum(hidden, 0.0).astype(bf16)
        return jnp.dot(hidden, out_w[cut, :], preferred_element_type=f32)

    @pl.when(step == 0)
    def _():
        piece(0).start()
        piece(1).start()
        tail().start()
        total = None
        for index in range(0, PARTS, 2):
            piece(index).wait()
            piece(index + 1).wait()
            if index == 0:
                tail().wait()
            if index + 2 < PARTS:
                piece(index + 2).start()
                piece(index + 3).start()
            term = layer(pl.ds(index * span, 2 * span))
            total = term if total is None else total + term
        finish(total)

    @pl.when(step > 0)
    def _():
        finish(layer(pl.ds(0, hidden_w.shape[1])))


def project(feat_map, w_hidden, w_out):
    height, columns, channels = feat_map.shape
    pixels = height * columns
    hidden, width = w_out.shape
    return pl.pallas_call(
        project_kernel,
        grid=(pixels // ROWS,),
        in_specs=[pl.BlockSpec((ROWS, channels), lambda i: (i, 0)), ANY, ANY],
        out_specs=pl.BlockSpec((ROWS, width), lambda i: (i, 0)),
        out_shape=jax.ShapeDtypeStruct((pixels, width), bf16),
        scratch_shapes=[
            pltpu.VMEM((channels, hidden), bf16),
            pltpu.VMEM((hidden, width), bf16),
            pltpu.SemaphoreType.DMA((PARTS + 1,)),
        ],
        compiler_params=pltpu.CompilerParams(vmem_limit_bytes=LIMIT),
        cost_estimate=pl.CostEstimate(
            flops=2 * pixels * hidden * (channels + width),
            bytes_accessed=2 * (pixels * channels + hidden * (channels + width)),
            transcendentals=0,
        ),
    )(feat_map.reshape(pixels, channels), w_hidden, w_out)


def pack_kernel(req_ref, keys_ref, out_ref, sem):
    for shard in range(out_ref.shape[0]):
        for rank in range(CAP):
            source = keys_ref.at[req_ref[shard, 0, rank]]
            pltpu.make_async_copy(source, out_ref.at[shard, rank], sem).start()
    pltpu.make_async_copy(out_ref, out_ref, sem).wait()


def pack(req, key_blocks):
    return pl.pallas_call(
        pack_kernel,
        in_specs=[SMEM, VMEM],
        out_specs=ANY,
        out_shape=jax.ShapeDtypeStruct((req.shape[0], CAP) + key_blocks.shape[1:], bf16),
        scratch_shapes=[pltpu.SemaphoreType.DMA],
        compiler_params=SMALL,
        name="pack_blocks",
    )(req, key_blocks)


def spread_kernel(own_ref, top_ref, bottom_ref, left_ref, right_ref, prop_ref, out_ref, rows_ref, side_ref, high_ref, low_ref, *, columns):
    pixels, _ = own_ref.shape
    sides = left_ref.shape[0]
    pad = side_ref.shape[0] // 2
    rows_ref[0:columns] = top_ref[...]
    rows_ref[columns : columns + pixels] = own_ref[...]
    rows_ref[columns + pixels :] = bottom_ref[...]
    side_ref[...] = jnp.zeros_like(side_ref)
    side_ref[0:sides] = left_ref[...]
    side_ref[pad : pad + sides] = right_ref[...]
    total = rows_ref.shape[0]
    weight = prop_ref[...]
    carried = jnp.dot(rows_ref[...], weight, preferred_element_type=f32)
    high = carried.astype(bf16)
    high_ref[0:total] = high
    low_ref[0:total] = (carried - high.astype(f32)).astype(bf16)
    carried = jnp.dot(side_ref[...], weight, preferred_element_type=f32)
    high = carried.astype(bf16)
    high_ref[total:] = high
    low_ref[total:] = (carried - high.astype(f32)).astype(bf16)

    size = 2 * columns
    reach = 4 * columns
    pix = lax.broadcasted_iota(jnp.int32, (size, reach), 0)
    oth = lax.broadcasted_iota(jnp.int32, (size, reach), 1)
    apart = oth // columns - pix // columns
    across = oth % columns - pix % columns
    near = (apart >= 0) & (apart <= 2) & (across >= -1) & (across <= 1)
    spix = lax.broadcasted_iota(jnp.int32, (size, 2 * pad), 0)
    soth = lax.broadcasted_iota(jnp.int32, (size, 2 * pad), 1)
    srow = jnp.where(soth < pad, soth, soth - pad) - spix // columns
    edge = jnp.where(soth < pad, 0, columns - 1) == spix % columns

    def weights(dots, keep):
        value = jnp.maximum(dots, 0.0)
        value = jnp.where(keep, value * value, 0.0)
        top = value.astype(bf16)
        return top, (value - top.astype(f32)).astype(bf16)

    def apply(pair, cut):
        top, rest = pair
        high, low = high_ref[cut], low_ref[cut]
        return (
            jnp.dot(top, high, preferred_element_type=f32)
            + jnp.dot(top, low, preferred_element_type=f32)
            + jnp.dot(rest, high, preferred_element_type=f32)
        )

    def block(index, carry):
        base = pl.multiple_of(index * size, size)
        own = own_ref[pl.ds(base, size)]
        around = pl.ds(base, reach)
        main = weights(transposed_dot(own, rows_ref[around]), near)
        shifted = srow - 2 * index
        keep = edge & (shifted >= 0) & (shifted <= 2)
        side = weights(transposed_dot(own, side_ref[...]), keep)
        spread = apply(main, around) + apply(side, pl.ds(total, 2 * pad))
        out_ref[pl.ds(base, size)] = normalize(spread).astype(bf16)
        return carry

    lax.fori_loop(0, pixels // size, block, 0)


def propagate(own, top, bottom, left, right, w_prop, columns):
    pixels, width = own.shape
    pad = -(-left.shape[0] // 16) * 16
    total = pixels + 2 * columns
    return pl.pallas_call(
        functools.partial(spread_kernel, columns=columns),
        in_specs=[VMEM] * 6,
        out_specs=VMEM,
        out_shape=jax.ShapeDtypeStruct((pixels, width), bf16),
        scratch_shapes=[
            pltpu.VMEM((total, width), bf16),
            pltpu.VMEM((2 * pad, width), bf16),
            pltpu.VMEM((total + 2 * pad, width), bf16),
            pltpu.VMEM((total + 2 * pad, width), bf16),
        ],
        compiler_params=SMALL,
        name="propagate",
    )(own, top, bottom, left, right, w_prop)


def loss_kernel(slot_ref, query_ref, keys_ref, partner_ref, mask_ref, out_ref):
    _, columns = out_ref.shape
    pixels, _ = query_ref.shape
    size = 2 * columns
    blocks = pixels // size
    per = slot_ref.shape[0] // blocks
    here = lax.broadcasted_iota(jnp.int32, (size, size), 0)
    there = lax.broadcasted_iota(jnp.int32, (size, size), 1)
    mirrored = (here // columns == there // columns) & (
        here % columns + there % columns == columns - 1
    )
    for block in range(blocks):
        query = query_ref[block * size : (block + 1) * size]
        match = transposed_dot(partner_ref[block * size : (block + 1) * size], query)
        match = jnp.sum(jnp.where(mirrored, match, 0.0), axis=0, keepdims=True)
        positive = match * inverse_divisor
        total = jnp.exp(positive)
        for n in range(per):
            keys = keys_ref[slot_ref[block * per + n]]
            logits = transposed_dot(keys, query) * inverse_divisor
            total = total + jnp.sum(jnp.exp(logits), axis=0, keepdims=True)
        loss = jnp.log(total) - positive
        for row in range(2):
            at = slice(2 * block + row, 2 * block + row + 1)
            piece = loss[:, row * columns : (row + 1) * columns]
            out_ref[at, :] = mask_ref[at, :].astype(f32) * piece


def loss_of(slot, query, received, partner, mask):
    return pl.pallas_call(
        loss_kernel,
        in_specs=[SMEM, VMEM, VMEM, VMEM, VMEM],
        out_specs=VMEM,
        out_shape=jax.ShapeDtypeStruct(mask.shape, f32),
        compiler_params=SMALL,
        name="loss_blocks",
    )(slot, query, received, partner, mask)


def shifted(value, axis):
    devices = lax.axis_size(axis)
    up = [(i, i + 1) for i in range(devices - 1)]
    return lax.ppermute(value[0], axis, up), lax.ppermute(value[1], axis, [(j, i) for i, j in up])


def per_device(feat_query, feat_key, w_hidden, w_out, w_prop, valid_mask, neg_shard, neg_block):
    height, columns, _ = feat_query.shape
    pixels = height * columns
    per_tile = pixels // 128
    shards = lax.axis_size("rows")
    cols = lax.axis_size("cols")
    want, slot = plan_slots(neg_shard, neg_block, shards)
    req = lax.all_to_all(want, "rows", 0, 0, tiled=True)
    key_map = project(feat_key, w_hidden, w_out)
    width = key_map.shape[-1]
    send = pack(req, key_map.reshape(per_tile, 128, width))
    received = lax.all_to_all(send, "rows", 0, 0, tiled=True)
    partner = lax.ppermute(key_map, "cols", [(i, cols - 1 - i) for i in range(cols)])
    feat_query, _ = lax.optimization_barrier((feat_query, send))
    query = project(feat_query, w_hidden, w_out)
    query_map = query.reshape(height, columns, width)
    top, bottom = shifted((query_map[-1], query_map[0]), "rows")
    first = jnp.concatenate([top[None, 0], query_map[:, 0], bottom[None, 0]])
    last = jnp.concatenate([top[None, -1], query_map[:, -1], bottom[None, -1]])
    left, right = shifted((last, first), "cols")
    propagated = propagate(query, top, bottom, left, right, w_prop, columns)
    return loss_of(
        slot, propagated, received.reshape(shards * CAP, 128, width), partner, valid_mask
    )


def solution(mesh):
    in_specs = (
        P("rows", "cols", None),
        P("rows", "cols", None),
        P(),
        P(),
        P(),
        P("rows", "cols"),
        P("rows", "cols", None, None),
        P("rows", "cols", None, None),
    )
    out_specs = P("rows", "cols")
    return jax.shard_map(
        per_device, mesh=mesh, in_specs=in_specs, out_specs=out_specs, check_vma=False
    )
```

```python
import functools

import jax
import jax.numpy as jnp
from jax import lax
from jax.experimental import pallas as pl
from jax.experimental.pallas import tpu as pltpu
from jax.sharding import PartitionSpec as P


epsilon = 1e-06
inverse_divisor = 10.0
CAP = 2
LANES = 128
VMEM = pl.BlockSpec(memory_space=pltpu.VMEM)
SMEM = pl.BlockSpec(memory_space=pltpu.SMEM)
ANY = pl.BlockSpec(memory_space=pl.ANY)
LIMIT = 60 * 2**20
SMALL = pltpu.CompilerParams(vmem_limit_bytes=12 * 2**20)
f32 = jnp.float32
bf16 = jnp.bfloat16


def normalize(vector):
    return vector * lax.rsqrt(jnp.sum(vector * vector, axis=-1, keepdims=True) + epsilon)


def transposed_dot(left, right):
    return lax.dot_general(left, right, (((1,), (1,)), ((), ())), preferred_element_type=f32)


def plan_kernel(shard_ref, block_ref, want_ref, slot_ref):
    _, _, per, blocks = shard_ref.shape
    shards = want_ref.shape[0]
    rows = lax.broadcasted_iota(jnp.int32, (shards, LANES), 0)
    lanes = lax.broadcasted_iota(jnp.int32, (shards, LANES), 1)
    want = jnp.zeros((shards, LANES), jnp.int32)
    chosen = []
    for block in range(blocks):
        for n in range(per):
            shard = shard_ref[0, 0, n, block]
            rank = jnp.int32(0)
            for other in chosen:
                rank = rank + (other == shard).astype(jnp.int32)
            rank = jnp.minimum(rank, CAP - 1)
            chosen.append(shard)
            slot_ref[block * per + n] = shard * CAP + rank
            want = jnp.where((rows == shard) & (lanes == rank), block_ref[0, 0, n, block], want)
    want_ref[...] = want.reshape(want_ref.shape)


def plan_slots(neg_shard, neg_block, shards):
    entries = neg_shard.size
    return pl.pallas_call(
        plan_kernel,
        in_specs=[SMEM, SMEM],
        out_specs=[VMEM, SMEM],
        out_shape=[
            jax.ShapeDtypeStruct((shards, 1, LANES), jnp.int32),
            jax.ShapeDtypeStruct((entries,), jnp.int32),
        ],
        compiler_params=SMALL,
        name="plan_slots",
    )(neg_shard.transpose(0, 1, 3, 2), neg_block.transpose(0, 1, 3, 2))


PARTS = 4
STRIP = 16


def project_kernel(*refs, edges):
    feat_hbm, hidden_hbm, out_hbm = refs[:3]
    if edges:
        other_hbm, map_ref, first_row, last_row, first_col, last_col = refs[3:9]
        feat, total, hidden_w, out_w, sems, strips = refs[9:]
        height, columns, _ = other_hbm.shape
    else:
        map_ref, feat, total, hidden_w, out_w, sems = refs[3:]
    pixels, channels = feat_hbm.shape
    half = pixels // 2
    span = channels // PARTS
    cuts = [slice(part * span, (part + 1) * span) for part in range(PARTS)]

    def copy(source, target, sem):
        return pltpu.make_async_copy(source, target, sems.at[sem])

    feats = [copy(feat_hbm.at[0:half, c], feat.at[0:half, c], i) for i, c in enumerate(cuts)]
    pieces = [copy(hidden_hbm.at[c], hidden_w.at[c], PARTS + i) for i, c in enumerate(cuts)]
    later = [
        copy(out_hbm, out_w, 2 * PARTS),
        copy(feat_hbm.at[half:pixels], feat.at[half:pixels], 2 * PARTS + 1),
    ]
    if edges:
        top = pixels + columns
        later += [
            copy(other_hbm.at[0], feat.at[pixels:top], 2 * PARTS + 2),
            copy(other_hbm.at[height - 1], feat.at[top : top + columns], 2 * PARTS + 3),
            copy(other_hbm.at[:, 0:STRIP], strips.at[0], 2 * PARTS + 4),
            copy(other_hbm.at[:, columns - STRIP : columns], strips.at[1], 2 * PARTS + 5),
        ]
    for first, second in zip(feats, pieces):
        first.start()
        second.start()
    for one in later:
        one.start()
    for part, cut in enumerate(cuts):
        feats[part].wait()
        pieces[part].wait()
        term = jnp.dot(feat[0:half, cut], hidden_w[cut, :], preferred_element_type=f32)
        if part == 0:
            total[...] = term
        elif part < PARTS - 1:
            total[...] += term
        else:
            hidden = jnp.maximum(total[...] + term, 0.0).astype(bf16)
    later[0].wait()
    raw = jnp.dot(hidden, out_w[...], preferred_element_type=f32)
    map_ref[0:half] = normalize(raw).astype(bf16)
    for one in later[1:]:
        one.wait()
    if edges:
        row = lax.broadcasted_iota(jnp.int32, (height, height * STRIP), 0)
        place = lax.broadcasted_iota(jnp.int32, (height, height * STRIP), 1)
        base = pixels + 2 * columns
        for side, offset in ((0, 0), (1, STRIP - 1)):
            pick = (place == row * STRIP + offset).astype(f32).astype(bf16)
            strip = strips[side].reshape(height * STRIP, channels)
            taken = jnp.dot(pick, strip, preferred_element_type=f32).astype(bf16)
            feat[base + side * height : base + (side + 1) * height] = taken
    hidden = jnp.dot(feat[half:], hidden_w[...], preferred_element_type=f32)
    hidden = jnp.maximum(hidden, 0.0).astype(bf16)
    done = normalize(jnp.dot(hidden, out_w[...], preferred_element_type=f32)).astype(bf16)
    map_ref[half:pixels] = done[0 : pixels - half]
    if edges:
        place = pixels - half
        for ref in (first_row, last_row, first_col, last_col):
            ref[...] = done[place : place + ref.shape[0]]
            place += ref.shape[0]


def project(feat_map, w_hidden, w_out, other=None):
    height, columns, channels = feat_map.shape
    pixels = height * columns
    hidden, width = w_out.shape
    operands = [feat_map.reshape(pixels, channels), w_hidden, w_out]
    outputs = [jax.ShapeDtypeStruct((pixels, width), bf16)]
    extra = 0
    scratch = []
    if other is not None:
        operands.append(other)
        for size in (columns, columns, height, height):
            outputs.append(jax.ShapeDtypeStruct((size, width), bf16))
            extra += size
        scratch = [pltpu.VMEM((2, height, STRIP, channels), bf16)]
    results = pl.pallas_call(
        functools.partial(project_kernel, edges=other is not None),
        in_specs=[ANY] * len(operands),
        out_specs=[VMEM] * len(outputs),
        out_shape=outputs,
        scratch_shapes=[
            pltpu.VMEM((pixels + extra, channels), bf16),
            pltpu.VMEM((pixels // 2, hidden), f32),
            pltpu.VMEM((channels, hidden), bf16),
            pltpu.VMEM((hidden, width), bf16),
            pltpu.SemaphoreType.DMA((2 * PARTS + 6,)),
            *scratch,
        ],
        compiler_params=pltpu.CompilerParams(vmem_limit_bytes=LIMIT),
        cost_estimate=pl.CostEstimate(
            flops=2 * (pixels + extra) * hidden * (channels + width),
            bytes_accessed=2 * (pixels * channels + hidden * (channels + width)),
            transcendentals=0,
        ),
    )(*operands)
    return results if other is not None else results[0]


def pack_kernel(req_ref, keys_ref, out_ref, sem):
    for shard in range(out_ref.shape[0]):
        for rank in range(CAP):
            source = keys_ref.at[req_ref[shard, 0, rank]]
            pltpu.make_async_copy(source, out_ref.at[shard, rank], sem).start()
    pltpu.make_async_copy(out_ref, out_ref, sem).wait()


def pack(req, key_blocks):
    return pl.pallas_call(
        pack_kernel,
        in_specs=[SMEM, VMEM],
        out_specs=ANY,
        out_shape=jax.ShapeDtypeStruct((req.shape[0], CAP) + key_blocks.shape[1:], bf16),
        scratch_shapes=[pltpu.SemaphoreType.DMA],
        compiler_params=SMALL,
        name="pack_blocks",
    )(req, key_blocks)


def spread_kernel(own_ref, top_ref, bottom_ref, left_ref, right_ref, prop_ref, out_ref, rows_ref, side_ref, high_ref, low_ref, *, columns):
    pixels, _ = own_ref.shape
    sides = left_ref.shape[0]
    pad = side_ref.shape[0] // 2
    rows_ref[0:columns] = top_ref[...]
    rows_ref[columns : columns + pixels] = own_ref[...]
    rows_ref[columns + pixels :] = bottom_ref[...]
    side_ref[...] = jnp.zeros_like(side_ref)
    side_ref[0:sides] = left_ref[...]
    side_ref[pad : pad + sides] = right_ref[...]
    total = rows_ref.shape[0]
    weight = prop_ref[...]
    carried = jnp.dot(rows_ref[...], weight, preferred_element_type=f32)
    high = carried.astype(bf16)
    high_ref[0:total] = high
    low_ref[0:total] = (carried - high.astype(f32)).astype(bf16)
    carried = jnp.dot(side_ref[...], weight, preferred_element_type=f32)
    high = carried.astype(bf16)
    high_ref[total:] = high
    low_ref[total:] = (carried - high.astype(f32)).astype(bf16)

    size = 2 * columns
    reach = 4 * columns
    pix = lax.broadcasted_iota(jnp.int32, (size, reach), 0)
    oth = lax.broadcasted_iota(jnp.int32, (size, reach), 1)
    apart = oth // columns - pix // columns
    across = oth % columns - pix % columns
    near = (apart >= 0) & (apart <= 2) & (across >= -1) & (across <= 1)
    spix = lax.broadcasted_iota(jnp.int32, (size, 2 * pad), 0)
    soth = lax.broadcasted_iota(jnp.int32, (size, 2 * pad), 1)
    srow = jnp.where(soth < pad, soth, soth - pad) - spix // columns
    edge = jnp.where(soth < pad, 0, columns - 1) == spix % columns

    def weights(dots, keep):
        value = jnp.maximum(dots, 0.0)
        value = jnp.where(keep, value * value, 0.0)
        top = value.astype(bf16)
        return top, (value - top.astype(f32)).astype(bf16)

    def apply(pair, cut):
        top, rest = pair
        high, low = high_ref[cut], low_ref[cut]
        return (
            jnp.dot(top, high, preferred_element_type=f32)
            + jnp.dot(top, low, preferred_element_type=f32)
            + jnp.dot(rest, high, preferred_element_type=f32)
        )

    def block(index, carry):
        base = pl.multiple_of(index * size, size)
        own = own_ref[pl.ds(base, size)]
        around = pl.ds(base, reach)
        main = weights(transposed_dot(own, rows_ref[around]), near)
        shifted = srow - 2 * index
        keep = edge & (shifted >= 0) & (shifted <= 2)
        side = weights(transposed_dot(own, side_ref[...]), keep)
        spread = apply(main, around) + apply(side, pl.ds(total, 2 * pad))
        out_ref[pl.ds(base, size)] = normalize(spread).astype(bf16)
        return carry

    lax.fori_loop(0, pixels // size, block, 0)


def propagate(own, top, bottom, left, right, w_prop, columns):
    pixels, width = own.shape
    pad = -(-left.shape[0] // 16) * 16
    total = pixels + 2 * columns
    return pl.pallas_call(
        functools.partial(spread_kernel, columns=columns),
        in_specs=[VMEM] * 6,
        out_specs=VMEM,
        out_shape=jax.ShapeDtypeStruct((pixels, width), bf16),
        scratch_shapes=[
            pltpu.VMEM((total, width), bf16),
            pltpu.VMEM((2 * pad, width), bf16),
            pltpu.VMEM((total + 2 * pad, width), bf16),
            pltpu.VMEM((total + 2 * pad, width), bf16),
        ],
        compiler_params=SMALL,
        name="propagate",
    )(own, top, bottom, left, right, w_prop)


def loss_kernel(slot_ref, query_ref, keys_ref, partner_ref, mask_ref, out_ref):
    _, columns = out_ref.shape
    pixels, _ = query_ref.shape
    size = 2 * columns
    blocks = pixels // size
    per = slot_ref.shape[0] // blocks
    here = lax.broadcasted_iota(jnp.int32, (size, size), 0)
    there = lax.broadcasted_iota(jnp.int32, (size, size), 1)
    mirrored = (here // columns == there // columns) & (
        here % columns + there % columns == columns - 1
    )
    for block in range(blocks):
        query = query_ref[block * size : (block + 1) * size]
        match = transposed_dot(partner_ref[block * size : (block + 1) * size], query)
        match = jnp.sum(jnp.where(mirrored, match, 0.0), axis=0, keepdims=True)
        positive = match * inverse_divisor
        total = jnp.exp(positive)
        for n in range(per):
            keys = keys_ref[slot_ref[block * per + n]]
            logits = transposed_dot(keys, query) * inverse_divisor
            total = total + jnp.sum(jnp.exp(logits), axis=0, keepdims=True)
        loss = jnp.log(total) - positive
        for row in range(2):
            at = slice(2 * block + row, 2 * block + row + 1)
            piece = loss[:, row * columns : (row + 1) * columns]
            out_ref[at, :] = mask_ref[at, :].astype(f32) * piece


def loss_of(slot, query, received, partner, mask):
    return pl.pallas_call(
        loss_kernel,
        in_specs=[SMEM, VMEM, VMEM, VMEM, VMEM],
        out_specs=VMEM,
        out_shape=jax.ShapeDtypeStruct(mask.shape, f32),
        compiler_params=SMALL,
        name="loss_blocks",
    )(slot, query, received, partner, mask)


def shifted(value, axis):
    devices = lax.axis_size(axis)
    up = [(i, i + 1) for i in range(devices - 1)]
    return lax.ppermute(value[0], axis, up), lax.ppermute(value[1], axis, [(j, i) for i, j in up])


def per_device(feat_query, feat_key, w_hidden, w_out, w_prop, valid_mask, neg_shard, neg_block):
    height, columns, _ = feat_query.shape
    pixels = height * columns
    per_tile = pixels // 128
    shards = lax.axis_size("rows")
    cols = lax.axis_size("cols")
    want, slot = plan_slots(neg_shard, neg_block, shards)
    req = lax.all_to_all(want, "rows", 0, 0, tiled=True)
    key_map, first_row, last_row, first_col, last_col = project(
        feat_key, w_hidden, w_out, feat_query
    )
    width = key_map.shape[-1]
    top, bottom = shifted((last_row, first_row), "rows")
    send = pack(req, key_map.reshape(per_tile, 128, width))
    received = lax.all_to_all(send, "rows", 0, 0, tiled=True)
    partner = lax.ppermute(key_map, "cols", [(i, cols - 1 - i) for i in range(cols)])
    first = jnp.concatenate([top[:1], first_col, bottom[:1]])
    last = jnp.concatenate([top[-1:], last_col, bottom[-1:]])
    left, right = shifted((last, first), "cols")
    feat_query, _ = lax.optimization_barrier((feat_query, send))
    query = project(feat_query, w_hidden, w_out)
    propagated = propagate(query, top, bottom, left, right, w_prop, columns)
    return loss_of(
        slot, propagated, received.reshape(shards * CAP, 128, width), partner, valid_mask
    )


def solution(mesh):
    in_specs = (
        P("rows", "cols", None),
        P("rows", "cols", None),
        P(),
        P(),
        P(),
        P("rows", "cols"),
        P("rows", "cols", None, None),
        P("rows", "cols", None, None),
    )
    out_specs = P("rows", "cols")
    return jax.shard_map(
        per_device, mesh=mesh, in_specs=in_specs, out_specs=out_specs, check_vma=False
    )
```

```python
import functools

import jax
import jax.numpy as jnp
from jax import lax
from jax.experimental import pallas as pl
from jax.experimental.pallas import tpu as pltpu
from jax.sharding import PartitionSpec as P


epsilon = 1e-06
inverse_divisor = 10.0
CAP = 2
LANES = 128
VMEM = pl.BlockSpec(memory_space=pltpu.VMEM)
SMEM = pl.BlockSpec(memory_space=pltpu.SMEM)
ANY = pl.BlockSpec(memory_space=pl.ANY)
LIMIT = 60 * 2**20
SMALL = pltpu.CompilerParams(vmem_limit_bytes=12 * 2**20)
WHOLE = pltpu.CompilerParams(vmem_limit_bytes=LIMIT)
f32 = jnp.float32
bf16 = jnp.bfloat16


def normalize(vector):
    return vector * lax.rsqrt(jnp.sum(vector * vector, axis=-1, keepdims=True) + epsilon)


def transposed_dot(left, right):
    return lax.dot_general(left, right, (((1,), (1,)), ((), ())), preferred_element_type=f32)


def plan_kernel(shard_any, block_any, want_ref, slot_ref, shard_ref, block_ref, sems):
    _, _, per, blocks = shard_ref.shape
    loads = [
        pltpu.make_async_copy(shard_any, shard_ref, sems.at[0]),
        pltpu.make_async_copy(block_any, block_ref, sems.at[1]),
    ]
    for load in loads:
        load.start()
    for load in loads:
        load.wait()
    shards = want_ref.shape[0]
    rows = lax.broadcasted_iota(jnp.int32, (shards, LANES), 0)
    lanes = lax.broadcasted_iota(jnp.int32, (shards, LANES), 1)
    want = jnp.zeros((shards, LANES), jnp.int32)
    chosen = []
    for block in range(blocks):
        for n in range(per):
            shard = shard_ref[0, 0, n, block]
            rank = jnp.int32(0)
            for other in chosen:
                rank = rank + (other == shard).astype(jnp.int32)
            rank = jnp.minimum(rank, CAP - 1)
            chosen.append(shard)
            slot_ref[block * per + n] = shard * CAP + rank
            want = jnp.where((rows == shard) & (lanes == rank), block_ref[0, 0, n, block], want)
    want_ref[...] = want.reshape(want_ref.shape)


def plan_slots(neg_shard, neg_block, shards):
    entries = neg_shard.size
    flipped = [array.transpose(0, 1, 3, 2) for array in (neg_shard, neg_block)]
    return pl.pallas_call(
        plan_kernel,
        in_specs=[ANY, ANY],
        out_specs=[VMEM, SMEM],
        scratch_shapes=[
            pltpu.SMEM(flipped[0].shape, jnp.int32),
            pltpu.SMEM(flipped[1].shape, jnp.int32),
            pltpu.SemaphoreType.DMA((2,)),
        ],
        out_shape=[
            jax.ShapeDtypeStruct((shards, 1, LANES), jnp.int32),
            jax.ShapeDtypeStruct((entries,), jnp.int32),
        ],
        compiler_params=WHOLE,
        name="plan_slots",
    )(*flipped)


PARTS = 4
PIECE = 16


def project_kernel(*refs, columns):
    feat_hbm, hidden_hbm, out_hbm, map_ref = refs[:4]
    edges = refs[4:-5]
    feat, total, hidden_w, out_w, sems = refs[-5:]
    pixels, channels = feat_hbm.shape
    half = pixels // 2
    span = channels // PARTS
    cuts = [slice(part * span, (part + 1) * span) for part in range(PARTS)]

    def copy(source, target, sem):
        return pltpu.make_async_copy(source, target, sems.at[sem])

    feats = [copy(feat_hbm.at[0:half, c], feat.at[0:half, c], i) for i, c in enumerate(cuts)]
    pieces = [copy(hidden_hbm.at[c], hidden_w.at[c], PARTS + i) for i, c in enumerate(cuts)]
    later = [
        copy(out_hbm, out_w, 2 * PARTS),
        copy(feat_hbm.at[half:pixels], feat.at[half:pixels], 2 * PARTS + 1),
    ]
    for first, second in zip(feats, pieces):
        first.start()
        second.start()
    for one in later:
        one.start()
    for part, cut in enumerate(cuts):
        feats[part].wait()
        pieces[part].wait()
        term = jnp.dot(feat[0:half, cut], hidden_w[cut, :], preferred_element_type=f32)
        if part == 0:
            total[...] = term
        elif part < PARTS - 1:
            total[...] += term
        else:
            hidden = jnp.maximum(total[...] + term, 0.0).astype(bf16)
    later[0].wait()
    raw = jnp.dot(hidden, out_w[...], preferred_element_type=f32)
    map_ref[0:half] = normalize(raw).astype(bf16)
    later[1].wait()
    hidden = jnp.dot(feat[half:], hidden_w[...], preferred_element_type=f32)
    hidden = jnp.maximum(hidden, 0.0).astype(bf16)
    raw = jnp.dot(hidden, out_w[...], preferred_element_type=f32)
    map_ref[half:pixels] = normalize(raw).astype(bf16)
    if edges:
        first_row, last_row, first_col, last_col, *corners = edges
        height = first_col.shape[0]
        end = pixels - columns
        first_row[...] = map_ref[0:columns]
        last_row[...] = map_ref[end:pixels]
        row = lax.broadcasted_iota(jnp.int32, (2 * height, pixels), 0)
        place = lax.broadcasted_iota(jnp.int32, (2 * height, pixels), 1)
        wanted = jnp.where(row < height, row * columns, (row - height + 1) * columns - 1)
        pick = (place == wanted).astype(f32).astype(bf16)
        taken = jnp.dot(pick, map_ref[...], preferred_element_type=f32).astype(bf16)
        first_col[...] = taken[0:height]
        last_col[...] = taken[height:]
        begins = (0, columns - PIECE, end, pixels - PIECE)
        for ref, begin in zip(corners, begins):
            ref[...] = map_ref[begin : begin + PIECE]


def project(feat_map, w_hidden, w_out, edges=False):
    height, columns, channels = feat_map.shape
    pixels = height * columns
    hidden, width = w_out.shape
    sizes = (pixels,)
    if edges:
        sizes += (columns, columns, height, height) + (PIECE,) * 4
    results = pl.pallas_call(
        functools.partial(project_kernel, columns=columns),
        in_specs=[ANY] * 3,
        out_specs=[VMEM] * len(sizes),
        out_shape=[jax.ShapeDtypeStruct((size, width), bf16) for size in sizes],
        scratch_shapes=[
            pltpu.VMEM((pixels, channels), bf16),
            pltpu.VMEM((pixels // 2, hidden), f32),
            pltpu.VMEM((channels, hidden), bf16),
            pltpu.VMEM((hidden, width), bf16),
            pltpu.SemaphoreType.DMA((2 * PARTS + 2,)),
        ],
        compiler_params=pltpu.CompilerParams(vmem_limit_bytes=LIMIT),
        cost_estimate=pl.CostEstimate(
            flops=2 * pixels * hidden * (channels + width),
            bytes_accessed=2 * (pixels * channels + hidden * (channels + width)),
            transcendentals=0,
        ),
    )(feat_map.reshape(pixels, channels), w_hidden, w_out)
    return results if edges else results[0]


def pack_kernel(req_ref, keys_any, out_ref, keys_ref, sem, load_sem):
    load = pltpu.make_async_copy(keys_any, keys_ref, load_sem)
    load.start()
    load.wait()
    for shard in range(out_ref.shape[0]):
        for rank in range(CAP):
            source = keys_ref.at[req_ref[shard, 0, rank]]
            pltpu.make_async_copy(source, out_ref.at[shard, rank], sem).start()
    pltpu.make_async_copy(out_ref, out_ref, sem).wait()


def pack(req, key_blocks):
    return pl.pallas_call(
        pack_kernel,
        in_specs=[SMEM, ANY],
        out_specs=ANY,
        out_shape=jax.ShapeDtypeStruct((req.shape[0], CAP) + key_blocks.shape[1:], bf16),
        scratch_shapes=[
            pltpu.VMEM(key_blocks.shape, bf16),
            pltpu.SemaphoreType.DMA,
            pltpu.SemaphoreType.DMA,
        ],
        compiler_params=WHOLE,
        name="pack_blocks",
    )(req, key_blocks)


def split(value):
    high = value.astype(bf16)
    return high, (value - high.astype(f32)).astype(bf16)


def weights(dots, keep):
    value = jnp.maximum(dots, 0.0)
    return split(jnp.where(keep, value * value, 0.0))


def weighted(pair, high, low):
    top, rest = pair
    return (
        jnp.dot(top, high, preferred_element_type=f32)
        + jnp.dot(top, low, preferred_element_type=f32)
        + jnp.dot(rest, high, preferred_element_type=f32)
    )


def spread_kernel(own_any, prop_ref, out_ref, same_ref, rows_ref, high_ref, low_ref, sem, *, columns):
    pixels, width = out_ref.shape
    end = columns + pixels
    load = pltpu.make_async_copy(own_any, rows_ref.at[columns:end], sem)
    load.start()
    rows_ref[0:columns] = jnp.zeros((columns, width), bf16)
    rows_ref[end:] = jnp.zeros((columns, width), bf16)
    size = 2 * columns
    reach = 4 * columns
    pix = lax.broadcasted_iota(jnp.int32, (size, reach), 0)
    oth = lax.broadcasted_iota(jnp.int32, (size, reach), 1)
    apart = oth // columns - pix // columns
    across = oth % columns - pix % columns
    near = (apart >= 0) & (apart <= 2) & (across >= -1) & (across <= 1)
    load.wait()
    carried = jnp.dot(rows_ref[...], prop_ref[...], preferred_element_type=f32)
    high_ref[...], low_ref[...] = split(carried)
    for block in range(pixels // size):
        base = block * size
        around = slice(base, base + reach)
        own = rows_ref[base + columns : base + columns + size]
        main = weights(transposed_dot(own, rows_ref[around]), near)
        same_ref[base : base + size] = own
        out_ref[base : base + size] = weighted(main, high_ref[around], low_ref[around])


def propagate(own, w_prop, columns):
    pixels, width = own.shape
    total = pixels + 2 * columns
    return pl.pallas_call(
        functools.partial(spread_kernel, columns=columns),
        in_specs=[ANY, VMEM],
        out_specs=[VMEM, VMEM],
        out_shape=[
            jax.ShapeDtypeStruct((pixels, width), f32),
            jax.ShapeDtypeStruct((pixels, width), bf16),
        ],
        scratch_shapes=[
            pltpu.VMEM((total, width), bf16),
            pltpu.VMEM((total, width), bf16),
            pltpu.VMEM((total, width), bf16),
            pltpu.SemaphoreType.DMA,
        ],
        compiler_params=SMALL,
        cost_estimate=pl.CostEstimate(
            flops=2 * 10**9, bytes_accessed=2 * 10**6, transcendentals=0
        ),
        name="propagate",
    )(own, w_prop)


def loss_kernel(
    slot_ref,
    own_ref,
    spread_ref,
    top_ref,
    bottom_ref,
    left_ref,
    right_ref,
    above_left,
    above_right,
    below_left,
    below_right,
    prop_ref,
    keys_ref,
    partner_ref,
    mask_ref,
    out_ref,
    halo_ref,
    high_ref,
    low_ref,
    query_ref,
):
    height, columns = out_ref.shape
    pixels, _ = own_ref.shape
    size = 2 * columns
    blocks = pixels // size
    per = slot_ref.shape[0] // blocks
    start = 2 * columns
    halo_ref[0:columns] = top_ref[...]
    halo_ref[columns:start] = bottom_ref[...]
    place = start
    for ref in (left_ref, right_ref, above_left, above_right, below_left, below_right):
        halo_ref[place : place + ref.shape[0]] = ref[...]
        place += ref.shape[0]
    carried = jnp.dot(halo_ref[...], prop_ref[...], preferred_element_type=f32)
    high_ref[...], low_ref[...] = split(carried)

    here = lax.broadcasted_iota(jnp.int32, (size, size), 0)
    there = lax.broadcasted_iota(jnp.int32, (size, size), 1)
    mirrored = (here // columns == there // columns) & (
        here % columns + there % columns == columns - 1
    )
    pix = lax.broadcasted_iota(jnp.int32, (size, columns), 0)
    oth = lax.broadcasted_iota(jnp.int32, (size, columns), 1)
    across = oth - pix % columns
    level = (across >= -1) & (across <= 1)
    side = place - start
    spix = lax.broadcasted_iota(jnp.int32, (size, side), 0)
    soth = lax.broadcasted_iota(jnp.int32, (size, side), 1)
    far = -4 * pixels
    srow = jnp.where(soth < height, soth, soth - height)
    scol = jnp.where(soth < height, -1, columns)
    lone = soth - 2 * height
    corners = ((PIECE - 1, -1, -1), (0, -1, columns), (PIECE - 1, height, -1), (0, height, columns))
    srow = jnp.where(lone >= 0, far, srow)
    for group, (offset, row, col) in enumerate(corners):
        here_it_is = lone == group * PIECE + offset
        srow = jnp.where(here_it_is, row, srow)
        scol = jnp.where(here_it_is, col, scol)
    srow = srow - spix // columns
    scol = scol - spix % columns
    edge = (scol >= -1) & (scol <= 1)

    for block in range(blocks):
        at = slice(block * size, (block + 1) * size)
        own = own_ref[at]
        spread = spread_ref[at]
        cuts = [(slice(start, place), None)]
        if block == 0:
            cuts.append((slice(0, columns), 0))
        if block == blocks - 1:
            cuts.append((slice(columns, start), 1))
        for cut, row in cuts:
            if row is None:
                keep = edge & (srow >= 2 * block - 1) & (srow <= 2 * block + 1)
            else:
                keep = level & (pix // columns == row)
            pair = weights(transposed_dot(own, halo_ref[cut]), keep)
            spread = spread + weighted(pair, high_ref[cut], low_ref[cut])
        query_ref[at] = normalize(spread).astype(bf16)
    for block in range(blocks):
        at = slice(block * size, (block + 1) * size)
        query = query_ref[at]
        match = transposed_dot(partner_ref[at], query)
        match = jnp.sum(jnp.where(mirrored, match, 0.0), axis=0, keepdims=True)
        positive = match * inverse_divisor
        total = jnp.exp(positive)
        for n in range(per):
            keys = keys_ref[slot_ref[block * per + n]]
            logits = transposed_dot(keys, query) * inverse_divisor
            total = total + jnp.sum(jnp.exp(logits), axis=0, keepdims=True)
        loss = jnp.log(total) - positive
        for row in range(2):
            line = slice(2 * block + row, 2 * block + row + 1)
            piece = loss[:, row * columns : (row + 1) * columns]
            out_ref[line, :] = mask_ref[line, :].astype(f32) * piece


def loss_of(slot, own, spread, halos, w_prop, received, partner, mask):
    width = own.shape[1]
    total = sum(halo.shape[0] for halo in halos)
    return pl.pallas_call(
        loss_kernel,
        in_specs=[SMEM] + [VMEM] * 14,
        out_specs=VMEM,
        out_shape=jax.ShapeDtypeStruct(mask.shape, f32),
        scratch_shapes=[pltpu.VMEM((total, width), bf16)] * 3 + [pltpu.VMEM(own.shape, bf16)],
        compiler_params=SMALL,
        name="loss_blocks",
    )(slot, own, spread, *halos, w_prop, received, partner, mask)


def moved(value, down, across):
    rows, cols = lax.axis_size("rows"), lax.axis_size("cols")
    pairs = []
    for row in range(rows):
        for col in range(cols):
            if 0 <= row + down < rows and 0 <= col + across < cols:
                pairs.append((row * cols + col, (row + down) * cols + col + across))
    return lax.ppermute(value, ("rows", "cols"), pairs)


def per_device(feat_query, feat_key, w_hidden, w_out, w_prop, valid_mask, neg_shard, neg_block):
    height, columns, _ = feat_query.shape
    pixels = height * columns
    per_tile = pixels // 128
    shards = lax.axis_size("rows")
    cols = lax.axis_size("cols")
    want, slot = plan_slots(neg_shard, neg_block, shards)
    req = lax.all_to_all(want, "rows", 0, 0, tiled=True)
    key_map = project(feat_key, w_hidden, w_out)
    width = key_map.shape[-1]
    partner = lax.ppermute(key_map, "cols", [(i, cols - 1 - i) for i in range(cols)])
    send = pack(req, key_map.reshape(per_tile, 128, width))
    received = lax.all_to_all(send, "rows", 0, 0, tiled=True)
    received = received.reshape(shards * CAP, 128, width)
    feat_query, _ = lax.optimization_barrier((feat_query, send))
    query, *edges = project(feat_query, w_hidden, w_out, True)
    first_row, last_row, first_col, last_col, *corners = edges
    steps = (
        (last_row, 1, 0),
        (first_row, -1, 0),
        (last_col, 0, 1),
        (first_col, 0, -1),
        (corners[3], 1, 1),
        (corners[2], 1, -1),
        (corners[1], -1, 1),
        (corners[0], -1, -1),
    )
    halos = [moved(value, down, across) for value, down, across in steps]
    spread, own = propagate(query, w_prop, columns)
    return loss_of(slot, own, spread, halos, w_prop, received, partner, valid_mask)


def solution(mesh):
    in_specs = (
        P("rows", "cols", None),
        P("rows", "cols", None),
        P(),
        P(),
        P(),
        P("rows", "cols"),
        P("rows", "cols", None, None),
        P("rows", "cols", None, None),
    )
    out_specs = P("rows", "cols")
    return jax.shard_map(
        per_device, mesh=mesh, in_specs=in_specs, out_specs=out_specs, check_vma=False
    )
```

```python
import functools

import jax
import jax.numpy as jnp
from jax import lax
from jax.experimental import pallas as pl
from jax.experimental.pallas import tpu as pltpu
from jax.sharding import PartitionSpec as P


epsilon = 1e-06
inverse_divisor = 10.0
CAP = 2
LANES = 128
VMEM = pl.BlockSpec(memory_space=pltpu.VMEM)
SMEM = pl.BlockSpec(memory_space=pltpu.SMEM)
ANY = pl.BlockSpec(memory_space=pl.ANY)
LIMIT = 60 * 2**20
SMALL = pltpu.CompilerParams(vmem_limit_bytes=12 * 2**20)
WHOLE = pltpu.CompilerParams(vmem_limit_bytes=LIMIT)
f32 = jnp.float32
bf16 = jnp.bfloat16


def normalize(vector):
    return vector * lax.rsqrt(jnp.sum(vector * vector, axis=-1, keepdims=True) + epsilon)


def transposed_dot(left, right):
    return lax.dot_general(left, right, (((1,), (1,)), ((), ())), preferred_element_type=f32)


def plan_kernel(shard_any, block_any, want_ref, slot_ref, shard_ref, block_ref, sems):
    _, _, per, blocks = shard_ref.shape
    loads = [
        pltpu.make_async_copy(shard_any, shard_ref, sems.at[0]),
        pltpu.make_async_copy(block_any, block_ref, sems.at[1]),
    ]
    for load in loads:
        load.start()
    for load in loads:
        load.wait()
    shards = want_ref.shape[0]
    rows = lax.broadcasted_iota(jnp.int32, (shards, LANES), 0)
    lanes = lax.broadcasted_iota(jnp.int32, (shards, LANES), 1)
    want = jnp.zeros((shards, LANES), jnp.int32)
    chosen = []
    for block in range(blocks):
        for n in range(per):
            shard = shard_ref[0, 0, n, block]
            rank = jnp.int32(0)
            for other in chosen:
                rank = rank + (other == shard).astype(jnp.int32)
            rank = jnp.minimum(rank, CAP - 1)
            chosen.append(shard)
            slot_ref[block * per + n] = shard * CAP + rank
            want = jnp.where((rows == shard) & (lanes == rank), block_ref[0, 0, n, block], want)
    want_ref[...] = want.reshape(want_ref.shape)


def plan_slots(neg_shard, neg_block, shards):
    entries = neg_shard.size
    flipped = [array.transpose(0, 1, 3, 2) for array in (neg_shard, neg_block)]
    return pl.pallas_call(
        plan_kernel,
        in_specs=[ANY, ANY],
        out_specs=[VMEM, SMEM],
        scratch_shapes=[
            pltpu.SMEM(flipped[0].shape, jnp.int32),
            pltpu.SMEM(flipped[1].shape, jnp.int32),
            pltpu.SemaphoreType.DMA((2,)),
        ],
        out_shape=[
            jax.ShapeDtypeStruct((shards, 1, LANES), jnp.int32),
            jax.ShapeDtypeStruct((entries,), jnp.int32),
        ],
        compiler_params=WHOLE,
        name="plan_slots",
    )(*flipped)


PARTS = 4


def project_kernel(*refs, columns):
    feat_hbm, hidden_hbm, out_hbm, map_ref = refs[:4]
    edges = refs[4:-5]
    feat, total, hidden_w, out_w, sems = refs[-5:]
    pixels, channels = feat_hbm.shape
    half = pixels // 2
    span = channels // PARTS
    cuts = [slice(part * span, (part + 1) * span) for part in range(PARTS)]

    def copy(source, target, sem):
        return pltpu.make_async_copy(source, target, sems.at[sem])

    feats = [copy(feat_hbm.at[0:half, c], feat.at[0:half, c], i) for i, c in enumerate(cuts)]
    pieces = [copy(hidden_hbm.at[c], hidden_w.at[c], PARTS + i) for i, c in enumerate(cuts)]
    later = [
        copy(out_hbm, out_w, 2 * PARTS),
        copy(feat_hbm.at[half:pixels], feat.at[half:pixels], 2 * PARTS + 1),
    ]
    for first, second in zip(feats, pieces):
        first.start()
        second.start()
    for one in later:
        one.start()
    for part, cut in enumerate(cuts):
        feats[part].wait()
        pieces[part].wait()
        term = jnp.dot(feat[0:half, cut], hidden_w[cut, :], preferred_element_type=f32)
        if part == 0:
            total[...] = term
        elif part < PARTS - 1:
            total[...] += term
        else:
            hidden = jnp.maximum(total[...] + term, 0.0).astype(bf16)
    later[0].wait()
    raw = jnp.dot(hidden, out_w[...], preferred_element_type=f32)
    map_ref[0:half] = normalize(raw).astype(bf16)
    later[1].wait()
    hidden = jnp.dot(feat[half:], hidden_w[...], preferred_element_type=f32)
    hidden = jnp.maximum(hidden, 0.0).astype(bf16)
    raw = jnp.dot(hidden, out_w[...], preferred_element_type=f32)
    map_ref[half:pixels] = normalize(raw).astype(bf16)
    if edges:
        first_row, last_row, first_col, last_col = edges
        height = first_col.shape[0]
        end = pixels - columns
        first_row[...] = map_ref[0:columns]
        last_row[...] = map_ref[end:pixels]
        row = lax.broadcasted_iota(jnp.int32, (2 * height, pixels), 0)
        place = lax.broadcasted_iota(jnp.int32, (2 * height, pixels), 1)
        wanted = jnp.where(row < height, row * columns, (row - height + 1) * columns - 1)
        pick = (place == wanted).astype(f32).astype(bf16)
        taken = jnp.dot(pick, map_ref[...], preferred_element_type=f32).astype(bf16)
        first_col[...] = taken[0:height]
        last_col[...] = taken[height:]


def project(feat_map, w_hidden, w_out, edges=False):
    height, columns, channels = feat_map.shape
    pixels = height * columns
    hidden, width = w_out.shape
    sizes = (pixels,)
    if edges:
        sizes += (columns, columns, height, height)
    results = pl.pallas_call(
        functools.partial(project_kernel, columns=columns),
        in_specs=[ANY] * 3,
        out_specs=[VMEM] * len(sizes),
        out_shape=[jax.ShapeDtypeStruct((size, width), bf16) for size in sizes],
        scratch_shapes=[
            pltpu.VMEM((pixels, channels), bf16),
            pltpu.VMEM((pixels // 2, hidden), f32),
            pltpu.VMEM((channels, hidden), bf16),
            pltpu.VMEM((hidden, width), bf16),
            pltpu.SemaphoreType.DMA((2 * PARTS + 2,)),
        ],
        compiler_params=pltpu.CompilerParams(vmem_limit_bytes=LIMIT),
        cost_estimate=pl.CostEstimate(
            flops=2 * pixels * hidden * (channels + width),
            bytes_accessed=2 * (pixels * channels + hidden * (channels + width)),
            transcendentals=0,
        ),
    )(feat_map.reshape(pixels, channels), w_hidden, w_out)
    return results if edges else results[0]


def pack_kernel(req_ref, keys_ref, out_ref, sem):
    for shard in range(out_ref.shape[0]):
        for rank in range(CAP):
            source = keys_ref.at[req_ref[shard, 0, rank]]
            pltpu.make_async_copy(source, out_ref.at[shard, rank], sem).start()
    pltpu.make_async_copy(out_ref, out_ref, sem).wait()


def pack(req, key_blocks):
    return pl.pallas_call(
        pack_kernel,
        in_specs=[SMEM, VMEM],
        out_specs=ANY,
        out_shape=jax.ShapeDtypeStruct((req.shape[0], CAP) + key_blocks.shape[1:], bf16),
        scratch_shapes=[pltpu.SemaphoreType.DMA],
        compiler_params=SMALL,
        name="pack_blocks",
    )(req, key_blocks)


def split(value):
    high = value.astype(bf16)
    return high, (value - high.astype(f32)).astype(bf16)


def weights(dots, keep):
    value = jnp.maximum(dots, 0.0)
    return split(jnp.where(keep, value * value, 0.0))


def weighted(pair, high, low):
    top, rest = pair
    return (
        jnp.dot(top, high, preferred_element_type=f32)
        + jnp.dot(top, low, preferred_element_type=f32)
        + jnp.dot(rest, high, preferred_element_type=f32)
    )


def spread_kernel(own_any, prop_ref, out_ref, rows_ref, high_ref, low_ref, sem, *, columns):
    pixels, width = out_ref.shape
    end = columns + pixels
    load = pltpu.make_async_copy(own_any, rows_ref.at[columns:end], sem)
    load.start()
    rows_ref[0:columns] = jnp.zeros((columns, width), bf16)
    rows_ref[end:] = jnp.zeros((columns, width), bf16)
    size = 2 * columns
    reach = 4 * columns
    pix = lax.broadcasted_iota(jnp.int32, (size, reach), 0)
    oth = lax.broadcasted_iota(jnp.int32, (size, reach), 1)
    apart = oth // columns - pix // columns
    across = oth % columns - pix % columns
    near = (apart >= 0) & (apart <= 2) & (across >= -1) & (across <= 1)
    load.wait()
    carried = jnp.dot(rows_ref[...], prop_ref[...], preferred_element_type=f32)
    high_ref[...], low_ref[...] = split(carried)
    for block in range(pixels // size):
        base = block * size
        around = slice(base, base + reach)
        own = rows_ref[base + columns : base + columns + size]
        main = weights(transposed_dot(own, rows_ref[around]), near)
        out_ref[base : base + size] = weighted(main, high_ref[around], low_ref[around])


def propagate(own, w_prop, columns):
    pixels, width = own.shape
    total = pixels + 2 * columns
    return pl.pallas_call(
        functools.partial(spread_kernel, columns=columns),
        in_specs=[ANY, VMEM],
        out_specs=VMEM,
        out_shape=jax.ShapeDtypeStruct((pixels, width), f32),
        scratch_shapes=[
            pltpu.VMEM((total, width), bf16),
            pltpu.VMEM((total, width), bf16),
            pltpu.VMEM((total, width), bf16),
            pltpu.SemaphoreType.DMA,
        ],
        compiler_params=SMALL,
        cost_estimate=pl.CostEstimate(
            flops=2 * 10**9, bytes_accessed=2 * 10**6, transcendentals=0
        ),
        name="propagate",
    )(own, w_prop)


def outside(own, halo_ref, high_ref, low_ref, cut, keep):
    pair = weights(transposed_dot(own, halo_ref[cut]), keep)
    return weighted(pair, high_ref[cut], low_ref[cut])


def loss_kernel(
    slot_ref,
    spread_ref,
    first_row,
    last_row,
    first_col,
    last_col,
    top_ref,
    bottom_ref,
    left_ref,
    right_ref,
    prop_ref,
    keys_ref,
    partner_ref,
    mask_ref,
    out_ref,
    halo_ref,
    high_ref,
    low_ref,
    query_ref,
):
    height, columns = out_ref.shape
    pixels, width = query_ref.shape
    size = 2 * columns
    blocks = pixels // size
    per = slot_ref.shape[0] // blocks
    sides = left_ref.shape[0]
    start = 2 * columns
    pad = (halo_ref.shape[0] - start) // 2
    halo_ref[start:] = jnp.zeros((2 * pad, width), bf16)
    halo_ref[0:columns] = top_ref[...]
    halo_ref[columns:start] = bottom_ref[...]
    halo_ref[start : start + sides] = left_ref[...]
    halo_ref[start + pad : start + pad + sides] = right_ref[...]
    carried = jnp.dot(halo_ref[...], prop_ref[...], preferred_element_type=f32)
    high_ref[...], low_ref[...] = split(carried)

    def gap(rows, lanes):
        mine = lax.broadcasted_iota(jnp.int32, (rows, lanes), 0)
        return lax.broadcasted_iota(jnp.int32, (rows, lanes), 1) - mine

    along = gap(columns, columns)
    level = (along >= -1) & (along <= 1)
    down = gap(height, pad)
    upright = (down >= 0) & (down <= 2)
    refs = (halo_ref, high_ref, low_ref)
    above = outside(first_row[...], *refs, slice(0, columns), level)
    below = outside(last_row[...], *refs, slice(columns, start), level)
    before = outside(first_col[...], *refs, slice(start, start + pad), upright)
    after = outside(last_col[...], *refs, slice(start + pad, start + 2 * pad), upright)

    here = lax.broadcasted_iota(jnp.int32, (size, size), 0)
    there = lax.broadcasted_iota(jnp.int32, (size, size), 1)
    mirrored = (here // columns == there // columns) & (
        here % columns + there % columns == columns - 1
    )
    column = lax.broadcasted_iota(jnp.int32, (columns, width), 0)
    for row in range(height):
        at = slice(row * columns, (row + 1) * columns)
        spread = spread_ref[at]
        spread = spread + jnp.where(column == 0, before[row : row + 1], 0.0)
        spread = spread + jnp.where(column == columns - 1, after[row : row + 1], 0.0)
        if row == 0:
            spread = spread + above
        if row == height - 1:
            spread = spread + below
        query_ref[at] = normalize(spread).astype(bf16)
    for block in range(blocks):
        at = slice(block * size, (block + 1) * size)
        query = query_ref[at]
        match = transposed_dot(partner_ref[at], query)
        match = jnp.sum(jnp.where(mirrored, match, 0.0), axis=0, keepdims=True)
        positive = match * inverse_divisor
        total = jnp.exp(positive)
        for n in range(per):
            keys = keys_ref[slot_ref[block * per + n]]
            logits = transposed_dot(keys, query) * inverse_divisor
            total = total + jnp.sum(jnp.exp(logits), axis=0, keepdims=True)
        loss = jnp.log(total) - positive
        for row in range(2):
            line = slice(2 * block + row, 2 * block + row + 1)
            piece = loss[:, row * columns : (row + 1) * columns]
            out_ref[line, :] = mask_ref[line, :].astype(f32) * piece


def loss_of(slot, spread, edges, halos, w_prop, received, partner, mask):
    columns = mask.shape[1]
    width = spread.shape[1]
    pad = -(-halos[2].shape[0] // 16) * 16
    total = 2 * columns + 2 * pad
    return pl.pallas_call(
        loss_kernel,
        in_specs=[SMEM] + [VMEM] * 13,
        out_specs=VMEM,
        out_shape=jax.ShapeDtypeStruct(mask.shape, f32),
        scratch_shapes=[pltpu.VMEM((total, width), bf16)] * 3 + [pltpu.VMEM(spread.shape, bf16)],
        compiler_params=SMALL,
        name="loss_blocks",
    )(slot, spread, *edges, *halos, w_prop, received, partner, mask)


def shifted(value, axis):
    devices = lax.axis_size(axis)
    up = [(i, i + 1) for i in range(devices - 1)]
    return lax.ppermute(value[0], axis, up), lax.ppermute(value[1], axis, [(j, i) for i, j in up])


def per_device(feat_query, feat_key, w_hidden, w_out, w_prop, valid_mask, neg_shard, neg_block):
    height, columns, _ = feat_query.shape
    pixels = height * columns
    per_tile = pixels // 128
    shards = lax.axis_size("rows")
    cols = lax.axis_size("cols")
    want, slot = plan_slots(neg_shard, neg_block, shards)
    req = lax.all_to_all(want, "rows", 0, 0, tiled=True)
    key_map = project(feat_key, w_hidden, w_out)
    width = key_map.shape[-1]
    partner = lax.ppermute(key_map, "cols", [(i, cols - 1 - i) for i in range(cols)])
    send = pack(req, key_map.reshape(per_tile, 128, width))
    received = lax.all_to_all(send, "rows", 0, 0, tiled=True)
    received = received.reshape(shards * CAP, 128, width)
    feat_query, _ = lax.optimization_barrier((feat_query, send))
    query, *edges = project(feat_query, w_hidden, w_out, True)
    first_row, last_row, first_col, last_col = edges
    top, bottom = shifted((last_row, first_row), "rows")
    first = jnp.concatenate([top[:1], first_col, bottom[:1]])
    last = jnp.concatenate([top[-1:], last_col, bottom[-1:]])
    left, right = shifted((last, first), "cols")
    halos = (top, bottom, left, right)
    spread = propagate(query, w_prop, columns)
    return loss_of(slot, spread, edges, halos, w_prop, received, partner, valid_mask)


def solution(mesh):
    in_specs = (
        P("rows", "cols", None),
        P("rows", "cols", None),
        P(),
        P(),
        P(),
        P("rows", "cols"),
        P("rows", "cols", None, None),
        P("rows", "cols", None, None),
    )
    out_specs = P("rows", "cols")
    return jax.shard_map(
        per_device, mesh=mesh, in_specs=in_specs, out_specs=out_specs, check_vma=False
    )
```

```python
import functools

import jax
import jax.numpy as jnp
from jax import lax
from jax.experimental import pallas as pl
from jax.experimental.pallas import tpu as pltpu
from jax.sharding import PartitionSpec as P


epsilon = 1e-06
inverse_divisor = 10.0
CAP = 2
LANES = 128
VMEM = pl.BlockSpec(memory_space=pltpu.VMEM)
SMEM = pl.BlockSpec(memory_space=pltpu.SMEM)
ANY = pl.BlockSpec(memory_space=pl.ANY)
LIMIT = 60 * 2**20
SMALL = pltpu.CompilerParams(vmem_limit_bytes=12 * 2**20)
WHOLE = pltpu.CompilerParams(vmem_limit_bytes=LIMIT)
f32 = jnp.float32
bf16 = jnp.bfloat16


def normalize(vector):
    return vector * lax.rsqrt(jnp.sum(vector * vector, axis=-1, keepdims=True) + epsilon)


def transposed_dot(left, right):
    return lax.dot_general(left, right, (((1,), (1,)), ((), ())), preferred_element_type=f32)


def plan_kernel(shard_any, block_any, want_ref, slot_ref, shard_ref, block_ref, sems):
    _, _, per, blocks = shard_ref.shape
    loads = [
        pltpu.make_async_copy(shard_any, shard_ref, sems.at[0]),
        pltpu.make_async_copy(block_any, block_ref, sems.at[1]),
    ]
    for load in loads:
        load.start()
    for load in loads:
        load.wait()
    shards = want_ref.shape[0]
    rows = lax.broadcasted_iota(jnp.int32, (shards, LANES), 0)
    lanes = lax.broadcasted_iota(jnp.int32, (shards, LANES), 1)
    want = jnp.zeros((shards, LANES), jnp.int32)
    chosen = []
    for block in range(blocks):
        for n in range(per):
            shard = shard_ref[0, 0, n, block]
            rank = jnp.int32(0)
            for other in chosen:
                rank = rank + (other == shard).astype(jnp.int32)
            rank = jnp.minimum(rank, CAP - 1)
            chosen.append(shard)
            slot_ref[block * per + n] = shard * CAP + rank
            want = jnp.where((rows == shard) & (lanes == rank), block_ref[0, 0, n, block], want)
    want_ref[...] = want.reshape(want_ref.shape)


def plan_slots(neg_shard, neg_block, shards):
    entries = neg_shard.size
    flipped = [array.transpose(0, 1, 3, 2) for array in (neg_shard, neg_block)]
    return pl.pallas_call(
        plan_kernel,
        in_specs=[ANY, ANY],
        out_specs=[VMEM, SMEM],
        scratch_shapes=[
            pltpu.SMEM(flipped[0].shape, jnp.int32),
            pltpu.SMEM(flipped[1].shape, jnp.int32),
            pltpu.SemaphoreType.DMA((2,)),
        ],
        out_shape=[
            jax.ShapeDtypeStruct((shards, 1, LANES), jnp.int32),
            jax.ShapeDtypeStruct((entries,), jnp.int32),
        ],
        compiler_params=WHOLE,
        name="plan_slots",
    )(*flipped)


PARTS = 4
FIRST = 4


def project_kernel(*refs, columns):
    feat_hbm, hidden_hbm, out_hbm, map_ref = refs[:4]
    edges = refs[4:-5]
    feat, total, hidden_w, out_w, sems = refs[-5:]
    pixels, channels = feat_hbm.shape
    half = pixels // FIRST
    span = channels // PARTS
    cuts = [slice(part * span, (part + 1) * span) for part in range(PARTS)]

    def copy(source, target, sem):
        return pltpu.make_async_copy(source, target, sems.at[sem])

    feats = [copy(feat_hbm.at[0:half, c], feat.at[0:half, c], i) for i, c in enumerate(cuts)]
    pieces = [copy(hidden_hbm.at[c], hidden_w.at[c], PARTS + i) for i, c in enumerate(cuts)]
    later = [
        copy(out_hbm, out_w, 2 * PARTS),
        copy(feat_hbm.at[half:pixels], feat.at[half:pixels], 2 * PARTS + 1),
    ]
    for first, second in zip(feats, pieces):
        first.start()
        second.start()
    for one in later:
        one.start()
    for part, cut in enumerate(cuts):
        feats[part].wait()
        pieces[part].wait()
        term = jnp.dot(feat[0:half, cut], hidden_w[cut, :], preferred_element_type=f32)
        if part == 0:
            total[...] = term
        elif part < PARTS - 1:
            total[...] += term
        else:
            hidden = jnp.maximum(total[...] + term, 0.0).astype(bf16)
    later[0].wait()
    raw = jnp.dot(hidden, out_w[...], preferred_element_type=f32)
    map_ref[0:half] = normalize(raw).astype(bf16)
    later[1].wait()
    hidden = jnp.dot(feat[half:], hidden_w[...], preferred_element_type=f32)
    hidden = jnp.maximum(hidden, 0.0).astype(bf16)
    raw = jnp.dot(hidden, out_w[...], preferred_element_type=f32)
    map_ref[half:pixels] = normalize(raw).astype(bf16)
    if edges:
        first_row, last_row, first_col, last_col = edges
        height = first_col.shape[0]
        end = pixels - columns
        first_row[...] = map_ref[0:columns]
        last_row[...] = map_ref[end:pixels]
        row = lax.broadcasted_iota(jnp.int32, (2 * height, pixels), 0)
        place = lax.broadcasted_iota(jnp.int32, (2 * height, pixels), 1)
        wanted = jnp.where(row < height, row * columns, (row - height + 1) * columns - 1)
        pick = (place == wanted).astype(f32).astype(bf16)
        taken = jnp.dot(pick, map_ref[...], preferred_element_type=f32).astype(bf16)
        first_col[...] = taken[0:height]
        last_col[...] = taken[height:]


def project(feat_map, w_hidden, w_out, edges=False):
    height, columns, channels = feat_map.shape
    pixels = height * columns
    hidden, width = w_out.shape
    sizes = (pixels,)
    if edges:
        sizes += (columns, columns, height, height)
    results = pl.pallas_call(
        functools.partial(project_kernel, columns=columns),
        in_specs=[ANY] * 3,
        out_specs=[VMEM] * len(sizes),
        out_shape=[jax.ShapeDtypeStruct((size, width), bf16) for size in sizes],
        scratch_shapes=[
            pltpu.VMEM((pixels, channels), bf16),
            pltpu.VMEM((pixels // FIRST, hidden), f32),
            pltpu.VMEM((channels, hidden), bf16),
            pltpu.VMEM((hidden, width), bf16),
            pltpu.SemaphoreType.DMA((2 * PARTS + 2,)),
        ],
        compiler_params=pltpu.CompilerParams(vmem_limit_bytes=LIMIT),
        cost_estimate=pl.CostEstimate(
            flops=2 * pixels * hidden * (channels + width),
            bytes_accessed=2 * (pixels * channels + hidden * (channels + width)),
            transcendentals=0,
        ),
    )(feat_map.reshape(pixels, channels), w_hidden, w_out)
    return results if edges else results[0]


def pack_kernel(req_ref, keys_ref, out_ref, sem):
    for shard in range(out_ref.shape[0]):
        for rank in range(CAP):
            source = keys_ref.at[req_ref[shard, 0, rank]]
            pltpu.make_async_copy(source, out_ref.at[shard, rank], sem).start()
    pltpu.make_async_copy(out_ref, out_ref, sem).wait()


def pack(req, key_blocks):
    return pl.pallas_call(
        pack_kernel,
        in_specs=[SMEM, VMEM],
        out_specs=ANY,
        out_shape=jax.ShapeDtypeStruct((req.shape[0], CAP) + key_blocks.shape[1:], bf16),
        scratch_shapes=[pltpu.SemaphoreType.DMA],
        compiler_params=SMALL,
        name="pack_blocks",
    )(req, key_blocks)


def split(value):
    high = value.astype(bf16)
    return high, (value - high.astype(f32)).astype(bf16)


def weights(dots, keep):
    value = jnp.maximum(dots, 0.0)
    return split(jnp.where(keep, value * value, 0.0))


def weighted(pair, high, low):
    top, rest = pair
    return (
        jnp.dot(top, high, preferred_element_type=f32)
        + jnp.dot(top, low, preferred_element_type=f32)
        + jnp.dot(rest, high, preferred_element_type=f32)
    )


def spread_kernel(own_any, prop_ref, out_ref, rows_ref, high_ref, low_ref, sem, *, columns):
    pixels, width = out_ref.shape
    end = columns + pixels
    load = pltpu.make_async_copy(own_any, rows_ref.at[columns:end], sem)
    load.start()
    rows_ref[0:columns] = jnp.zeros((columns, width), bf16)
    rows_ref[end:] = jnp.zeros((columns, width), bf16)
    size = 2 * columns
    reach = 4 * columns
    pix = lax.broadcasted_iota(jnp.int32, (size, reach), 0)
    oth = lax.broadcasted_iota(jnp.int32, (size, reach), 1)
    apart = oth // columns - pix // columns
    across = oth % columns - pix % columns
    near = (apart >= 0) & (apart <= 2) & (across >= -1) & (across <= 1)
    load.wait()
    carried = jnp.dot(rows_ref[...], prop_ref[...], preferred_element_type=f32)
    high_ref[...], low_ref[...] = split(carried)
    for block in range(pixels // size):
        base = block * size
        around = slice(base, base + reach)
        own = rows_ref[base + columns : base + columns + size]
        main = weights(transposed_dot(own, rows_ref[around]), near)
        out_ref[base : base + size] = weighted(main, high_ref[around], low_ref[around])


def propagate(own, w_prop, columns):
    pixels, width = own.shape
    total = pixels + 2 * columns
    return pl.pallas_call(
        functools.partial(spread_kernel, columns=columns),
        in_specs=[ANY, VMEM],
        out_specs=VMEM,
        out_shape=jax.ShapeDtypeStruct((pixels, width), f32),
        scratch_shapes=[
            pltpu.VMEM((total, width), bf16),
            pltpu.VMEM((total, width), bf16),
            pltpu.VMEM((total, width), bf16),
            pltpu.SemaphoreType.DMA,
        ],
        compiler_params=SMALL,
        cost_estimate=pl.CostEstimate(
            flops=2 * 10**9, bytes_accessed=2 * 10**6, transcendentals=0
        ),
        name="propagate",
    )(own, w_prop)


def outside(own, halo_ref, high_ref, low_ref, cut, keep):
    pair = weights(transposed_dot(own, halo_ref[cut]), keep)
    return weighted(pair, high_ref[cut], low_ref[cut])


def loss_kernel(
    slot_ref,
    spread_ref,
    first_row,
    last_row,
    first_col,
    last_col,
    top_ref,
    bottom_ref,
    left_ref,
    right_ref,
    prop_ref,
    keys_ref,
    partner_ref,
    mask_ref,
    out_ref,
    halo_ref,
    high_ref,
    low_ref,
    query_ref,
):
    height, columns = out_ref.shape
    pixels, width = query_ref.shape
    size = 2 * columns
    blocks = pixels // size
    per = slot_ref.shape[0] // blocks
    sides = left_ref.shape[0]
    start = 2 * columns
    pad = (halo_ref.shape[0] - start) // 2
    halo_ref[start:] = jnp.zeros((2 * pad, width), bf16)
    halo_ref[0:columns] = top_ref[...]
    halo_ref[columns:start] = bottom_ref[...]
    halo_ref[start : start + sides] = left_ref[...]
    halo_ref[start + pad : start + pad + sides] = right_ref[...]
    carried = jnp.dot(halo_ref[...], prop_ref[...], preferred_element_type=f32)
    high_ref[...], low_ref[...] = split(carried)

    def gap(rows, lanes):
        mine = lax.broadcasted_iota(jnp.int32, (rows, lanes), 0)
        return lax.broadcasted_iota(jnp.int32, (rows, lanes), 1) - mine

    along = gap(columns, columns)
    level = (along >= -1) & (along <= 1)
    down = gap(height, pad)
    upright = (down >= 0) & (down <= 2)
    refs = (halo_ref, high_ref, low_ref)
    above = outside(first_row[...], *refs, slice(0, columns), level)
    below = outside(last_row[...], *refs, slice(columns, start), level)
    before = outside(first_col[...], *refs, slice(start, start + pad), upright)
    after = outside(last_col[...], *refs, slice(start + pad, start + 2 * pad), upright)

    here = lax.broadcasted_iota(jnp.int32, (size, size), 0)
    there = lax.broadcasted_iota(jnp.int32, (size, size), 1)
    mirrored = (here // columns == there // columns) & (
        here % columns + there % columns == columns - 1
    )
    column = lax.broadcasted_iota(jnp.int32, (columns, width), 0)
    for row in range(height):
        at = slice(row * columns, (row + 1) * columns)
        spread = spread_ref[at]
        spread = spread + jnp.where(column == 0, before[row : row + 1], 0.0)
        spread = spread + jnp.where(column == columns - 1, after[row : row + 1], 0.0)
        if row == 0:
            spread = spread + above
        if row == height - 1:
            spread = spread + below
        query_ref[at] = normalize(spread).astype(bf16)
    for block in range(blocks):
        at = slice(block * size, (block + 1) * size)
        query = query_ref[at]
        match = transposed_dot(partner_ref[at], query)
        match = jnp.sum(jnp.where(mirrored, match, 0.0), axis=0, keepdims=True)
        positive = match * inverse_divisor
        total = jnp.exp(positive)
        for n in range(per):
            keys = keys_ref[slot_ref[block * per + n]]
            logits = transposed_dot(keys, query) * inverse_divisor
            total = total + jnp.sum(jnp.exp(logits), axis=0, keepdims=True)
        loss = jnp.log(total) - positive
        for row in range(2):
            line = slice(2 * block + row, 2 * block + row + 1)
            piece = loss[:, row * columns : (row + 1) * columns]
            out_ref[line, :] = mask_ref[line, :].astype(f32) * piece


def loss_of(slot, spread, edges, halos, w_prop, received, partner, mask):
    columns = mask.shape[1]
    width = spread.shape[1]
    pad = -(-halos[2].shape[0] // 16) * 16
    total = 2 * columns + 2 * pad
    return pl.pallas_call(
        loss_kernel,
        in_specs=[SMEM] + [VMEM] * 13,
        out_specs=VMEM,
        out_shape=jax.ShapeDtypeStruct(mask.shape, f32),
        scratch_shapes=[pltpu.VMEM((total, width), bf16)] * 3 + [pltpu.VMEM(spread.shape, bf16)],
        compiler_params=SMALL,
        name="loss_blocks",
    )(slot, spread, *edges, *halos, w_prop, received, partner, mask)


def shifted(value, axis):
    devices = lax.axis_size(axis)
    up = [(i, i + 1) for i in range(devices - 1)]
    return lax.ppermute(value[0], axis, up), lax.ppermute(value[1], axis, [(j, i) for i, j in up])


def per_device(feat_query, feat_key, w_hidden, w_out, w_prop, valid_mask, neg_shard, neg_block):
    height, columns, _ = feat_query.shape
    pixels = height * columns
    per_tile = pixels // 128
    shards = lax.axis_size("rows")
    cols = lax.axis_size("cols")
    want, slot = plan_slots(neg_shard, neg_block, shards)
    req = lax.all_to_all(want, "rows", 0, 0, tiled=True)
    key_map = project(feat_key, w_hidden, w_out)
    width = key_map.shape[-1]
    partner = lax.ppermute(key_map, "cols", [(i, cols - 1 - i) for i in range(cols)])
    send = pack(req, key_map.reshape(per_tile, 128, width))
    received = lax.all_to_all(send, "rows", 0, 0, tiled=True)
    received = received.reshape(shards * CAP, 128, width)
    feat_query, _ = lax.optimization_barrier((feat_query, send))
    query, *edges = project(feat_query, w_hidden, w_out, True)
    first_row, last_row, first_col, last_col = edges
    top, bottom = shifted((last_row, first_row), "rows")
    first = jnp.concatenate([top[:1], first_col, bottom[:1]])
    last = jnp.concatenate([top[-1:], last_col, bottom[-1:]])
    left, right = shifted((last, first), "cols")
    halos = (top, bottom, left, right)
    spread = propagate(query, w_prop, columns)
    return loss_of(slot, spread, edges, halos, w_prop, received, partner, valid_mask)


def solution(mesh):
    in_specs = (
        P("rows", "cols", None),
        P("rows", "cols", None),
        P(),
        P(),
        P(),
        P("rows", "cols"),
        P("rows", "cols", None, None),
        P("rows", "cols", None, None),
    )
    out_specs = P("rows", "cols")
    return jax.shard_map(
        per_device, mesh=mesh, in_specs=in_specs, out_specs=out_specs, check_vma=False
    )
```

```python
import functools

import jax
import jax.numpy as jnp
from jax import lax
from jax.experimental import pallas as pl
from jax.experimental.pallas import tpu as pltpu
from jax.sharding import PartitionSpec as P


epsilon = 1e-06
inverse_divisor = 10.0
CAP = 2
LANES = 128
VMEM = pl.BlockSpec(memory_space=pltpu.VMEM)
SMEM = pl.BlockSpec(memory_space=pltpu.SMEM)
ANY = pl.BlockSpec(memory_space=pl.ANY)
LIMIT = 60 * 2**20
SMALL = pltpu.CompilerParams(vmem_limit_bytes=12 * 2**20)
WHOLE = pltpu.CompilerParams(vmem_limit_bytes=LIMIT)
f32 = jnp.float32
bf16 = jnp.bfloat16


def normalize(vector):
    return vector * lax.rsqrt(jnp.sum(vector * vector, axis=-1, keepdims=True) + epsilon)


def transposed_dot(left, right):
    return lax.dot_general(left, right, (((1,), (1,)), ((), ())), preferred_element_type=f32)


def plan_kernel(shard_any, block_any, want_ref, slot_ref, shard_ref, block_ref, sems):
    _, _, per, blocks = shard_ref.shape
    loads = [
        pltpu.make_async_copy(shard_any, shard_ref, sems.at[0]),
        pltpu.make_async_copy(block_any, block_ref, sems.at[1]),
    ]
    for load in loads:
        load.start()
    for load in loads:
        load.wait()
    shards = want_ref.shape[0]
    rows = lax.broadcasted_iota(jnp.int32, (shards, LANES), 0)
    lanes = lax.broadcasted_iota(jnp.int32, (shards, LANES), 1)
    want = jnp.zeros((shards, LANES), jnp.int32)
    chosen = []
    for block in range(blocks):
        for n in range(per):
            shard = shard_ref[0, 0, n, block]
            rank = jnp.int32(0)
            for other in chosen:
                rank = rank + (other == shard).astype(jnp.int32)
            rank = jnp.minimum(rank, CAP - 1)
            chosen.append(shard)
            slot_ref[block * per + n] = shard * CAP + rank
            want = jnp.where((rows == shard) & (lanes == rank), block_ref[0, 0, n, block], want)
    want_ref[...] = want.reshape(want_ref.shape)


def plan_slots(neg_shard, neg_block, shards):
    entries = neg_shard.size
    flipped = [array.transpose(0, 1, 3, 2) for array in (neg_shard, neg_block)]
    return pl.pallas_call(
        plan_kernel,
        in_specs=[ANY, ANY],
        out_specs=[VMEM, SMEM],
        scratch_shapes=[
            pltpu.SMEM(flipped[0].shape, jnp.int32),
            pltpu.SMEM(flipped[1].shape, jnp.int32),
            pltpu.SemaphoreType.DMA((2,)),
        ],
        out_shape=[
            jax.ShapeDtypeStruct((shards, 1, LANES), jnp.int32),
            jax.ShapeDtypeStruct((entries,), jnp.int32),
        ],
        compiler_params=WHOLE,
        name="plan_slots",
    )(*flipped)


PARTS = 4
FIRST = 4


def project_kernel(*refs, columns):
    feat_hbm, hidden_hbm, out_hbm, map_ref = refs[:4]
    edges = refs[4:-5]
    feat, total, hidden_w, out_w, sems = refs[-5:]
    pixels, channels = feat_hbm.shape
    half = pixels // FIRST
    span = channels // PARTS
    cuts = [slice(part * span, (part + 1) * span) for part in range(PARTS)]

    def copy(source, target, sem):
        return pltpu.make_async_copy(source, target, sems.at[sem])

    feats = [copy(feat_hbm.at[0:half, c], feat.at[0:half, c], i) for i, c in enumerate(cuts)]
    pieces = [copy(hidden_hbm.at[c], hidden_w.at[c], PARTS + i) for i, c in enumerate(cuts)]
    bounds = (half, pixels // 2, pixels)
    spans = [slice(low, high) for low, high in zip(bounds, bounds[1:])]
    later = [copy(out_hbm, out_w, 2 * PARTS)]
    later += [copy(feat_hbm.at[c], feat.at[c], 2 * PARTS + 1 + i) for i, c in enumerate(spans)]
    for first, second in zip(feats, pieces):
        first.start()
        second.start()
    for one in later:
        one.start()
    for part, cut in enumerate(cuts):
        feats[part].wait()
        pieces[part].wait()
        term = jnp.dot(feat[0:half, cut], hidden_w[cut, :], preferred_element_type=f32)
        if part == 0:
            total[...] = term
        elif part < PARTS - 1:
            total[...] += term
        else:
            hidden = jnp.maximum(total[...] + term, 0.0).astype(bf16)
    later[0].wait()
    raw = jnp.dot(hidden, out_w[...], preferred_element_type=f32)
    map_ref[0:half] = normalize(raw).astype(bf16)
    for load, cut in zip(later[1:], spans):
        load.wait()
        hidden = jnp.dot(feat[cut], hidden_w[...], preferred_element_type=f32)
        hidden = jnp.maximum(hidden, 0.0).astype(bf16)
        raw = jnp.dot(hidden, out_w[...], preferred_element_type=f32)
        map_ref[cut] = normalize(raw).astype(bf16)
    if edges:
        first_row, last_row, first_col, last_col = edges
        height = first_col.shape[0]
        end = pixels - columns
        first_row[...] = map_ref[0:columns]
        last_row[...] = map_ref[end:pixels]
        row = lax.broadcasted_iota(jnp.int32, (2 * height, pixels), 0)
        place = lax.broadcasted_iota(jnp.int32, (2 * height, pixels), 1)
        wanted = jnp.where(row < height, row * columns, (row - height + 1) * columns - 1)
        pick = (place == wanted).astype(f32).astype(bf16)
        taken = jnp.dot(pick, map_ref[...], preferred_element_type=f32).astype(bf16)
        first_col[...] = taken[0:height]
        last_col[...] = taken[height:]


def project(feat_map, w_hidden, w_out, edges=False):
    height, columns, channels = feat_map.shape
    pixels = height * columns
    hidden, width = w_out.shape
    sizes = (pixels,)
    if edges:
        sizes += (columns, columns, height, height)
    results = pl.pallas_call(
        functools.partial(project_kernel, columns=columns),
        in_specs=[ANY] * 3,
        out_specs=[VMEM] * len(sizes),
        out_shape=[jax.ShapeDtypeStruct((size, width), bf16) for size in sizes],
        scratch_shapes=[
            pltpu.VMEM((pixels, channels), bf16),
            pltpu.VMEM((pixels // FIRST, hidden), f32),
            pltpu.VMEM((channels, hidden), bf16),
            pltpu.VMEM((hidden, width), bf16),
            pltpu.SemaphoreType.DMA((2 * PARTS + 3,)),
        ],
        compiler_params=pltpu.CompilerParams(vmem_limit_bytes=LIMIT),
        cost_estimate=pl.CostEstimate(
            flops=2 * pixels * hidden * (channels + width),
            bytes_accessed=2 * (pixels * channels + hidden * (channels + width)),
            transcendentals=0,
        ),
    )(feat_map.reshape(pixels, channels), w_hidden, w_out)
    return results if edges else results[0]


def pack_kernel(req_ref, keys_ref, out_ref, sem):
    for shard in range(out_ref.shape[0]):
        for rank in range(CAP):
            source = keys_ref.at[req_ref[shard, 0, rank]]
            pltpu.make_async_copy(source, out_ref.at[shard, rank], sem).start()
    pltpu.make_async_copy(out_ref, out_ref, sem).wait()


def pack(req, key_blocks):
    return pl.pallas_call(
        pack_kernel,
        in_specs=[SMEM, VMEM],
        out_specs=ANY,
        out_shape=jax.ShapeDtypeStruct((req.shape[0], CAP) + key_blocks.shape[1:], bf16),
        scratch_shapes=[pltpu.SemaphoreType.DMA],
        compiler_params=SMALL,
        name="pack_blocks",
    )(req, key_blocks)


def split(value):
    high = value.astype(bf16)
    return high, (value - high.astype(f32)).astype(bf16)


def weights(dots, keep):
    value = jnp.maximum(dots, 0.0)
    return split(jnp.where(keep, value * value, 0.0))


def weighted(pair, high, low):
    top, rest = pair
    return (
        jnp.dot(top, high, preferred_element_type=f32)
        + jnp.dot(top, low, preferred_element_type=f32)
        + jnp.dot(rest, high, preferred_element_type=f32)
    )


def spread_kernel(own_any, prop_ref, out_ref, rows_ref, high_ref, low_ref, sem, *, columns):
    pixels, width = out_ref.shape
    end = columns + pixels
    load = pltpu.make_async_copy(own_any, rows_ref.at[columns:end], sem)
    load.start()
    rows_ref[0:columns] = jnp.zeros((columns, width), bf16)
    rows_ref[end:] = jnp.zeros((columns, width), bf16)
    size = 2 * columns
    reach = 4 * columns
    pix = lax.broadcasted_iota(jnp.int32, (size, reach), 0)
    oth = lax.broadcasted_iota(jnp.int32, (size, reach), 1)
    apart = oth // columns - pix // columns
    across = oth % columns - pix % columns
    near = (apart >= 0) & (apart <= 2) & (across >= -1) & (across <= 1)
    load.wait()
    carried = jnp.dot(rows_ref[...], prop_ref[...], preferred_element_type=f32)
    high_ref[...], low_ref[...] = split(carried)
    for block in range(pixels // size):
        base = block * size
        around = slice(base, base + reach)
        own = rows_ref[base + columns : base + columns + size]
        main = weights(transposed_dot(own, rows_ref[around]), near)
        out_ref[base : base + size] = weighted(main, high_ref[around], low_ref[around])


def propagate(own, w_prop, columns):
    pixels, width = own.shape
    total = pixels + 2 * columns
    return pl.pallas_call(
        functools.partial(spread_kernel, columns=columns),
        in_specs=[ANY, VMEM],
        out_specs=VMEM,
        out_shape=jax.ShapeDtypeStruct((pixels, width), f32),
        scratch_shapes=[
            pltpu.VMEM((total, width), bf16),
            pltpu.VMEM((total, width), bf16),
            pltpu.VMEM((total, width), bf16),
            pltpu.SemaphoreType.DMA,
        ],
        compiler_params=SMALL,
        cost_estimate=pl.CostEstimate(
            flops=2 * 10**9, bytes_accessed=2 * 10**6, transcendentals=0
        ),
        name="propagate",
    )(own, w_prop)


def outside(own, halo_ref, high_ref, low_ref, cut, keep):
    pair = weights(transposed_dot(own, halo_ref[cut]), keep)
    return weighted(pair, high_ref[cut], low_ref[cut])


def loss_kernel(
    slot_ref,
    spread_ref,
    first_row,
    last_row,
    first_col,
    last_col,
    top_ref,
    bottom_ref,
    left_ref,
    right_ref,
    prop_ref,
    keys_ref,
    partner_ref,
    mask_ref,
    out_ref,
    halo_ref,
    high_ref,
    low_ref,
    query_ref,
):
    height, columns = out_ref.shape
    pixels, width = query_ref.shape
    size = 2 * columns
    blocks = pixels // size
    per = slot_ref.shape[0] // blocks
    sides = left_ref.shape[0]
    start = 2 * columns
    pad = (halo_ref.shape[0] - start) // 2
    halo_ref[start:] = jnp.zeros((2 * pad, width), bf16)
    halo_ref[0:columns] = top_ref[...]
    halo_ref[columns:start] = bottom_ref[...]
    halo_ref[start : start + sides] = left_ref[...]
    halo_ref[start + pad : start + pad + sides] = right_ref[...]
    carried = jnp.dot(halo_ref[...], prop_ref[...], preferred_element_type=f32)
    high_ref[...], low_ref[...] = split(carried)

    def gap(rows, lanes):
        mine = lax.broadcasted_iota(jnp.int32, (rows, lanes), 0)
        return lax.broadcasted_iota(jnp.int32, (rows, lanes), 1) - mine

    along = gap(columns, columns)
    level = (along >= -1) & (along <= 1)
    down = gap(height, pad)
    upright = (down >= 0) & (down <= 2)
    refs = (halo_ref, high_ref, low_ref)
    above = outside(first_row[...], *refs, slice(0, columns), level)
    below = outside(last_row[...], *refs, slice(columns, start), level)
    before = outside(first_col[...], *refs, slice(start, start + pad), upright)
    after = outside(last_col[...], *refs, slice(start + pad, start + 2 * pad), upright)

    here = lax.broadcasted_iota(jnp.int32, (size, size), 0)
    there = lax.broadcasted_iota(jnp.int32, (size, size), 1)
    mirrored = (here // columns == there // columns) & (
        here % columns + there % columns == columns - 1
    )
    column = lax.broadcasted_iota(jnp.int32, (columns, width), 0)
    for row in range(height):
        at = slice(row * columns, (row + 1) * columns)
        spread = spread_ref[at]
        spread = spread + jnp.where(column == 0, before[row : row + 1], 0.0)
        spread = spread + jnp.where(column == columns - 1, after[row : row + 1], 0.0)
        if row == 0:
            spread = spread + above
        if row == height - 1:
            spread = spread + below
        query_ref[at] = normalize(spread).astype(bf16)
    for block in range(blocks):
        at = slice(block * size, (block + 1) * size)
        query = query_ref[at]
        match = transposed_dot(partner_ref[at], query)
        match = jnp.sum(jnp.where(mirrored, match, 0.0), axis=0, keepdims=True)
        positive = match * inverse_divisor
        total = jnp.exp(positive)
        for n in range(per):
            keys = keys_ref[slot_ref[block * per + n]]
            logits = transposed_dot(keys, query) * inverse_divisor
            total = total + jnp.sum(jnp.exp(logits), axis=0, keepdims=True)
        loss = jnp.log(total) - positive
        for row in range(2):
            line = slice(2 * block + row, 2 * block + row + 1)
            piece = loss[:, row * columns : (row + 1) * columns]
            out_ref[line, :] = mask_ref[line, :].astype(f32) * piece


def loss_of(slot, spread, edges, halos, w_prop, received, partner, mask):
    columns = mask.shape[1]
    width = spread.shape[1]
    pad = -(-halos[2].shape[0] // 16) * 16
    total = 2 * columns + 2 * pad
    return pl.pallas_call(
        loss_kernel,
        in_specs=[SMEM] + [VMEM] * 13,
        out_specs=VMEM,
        out_shape=jax.ShapeDtypeStruct(mask.shape, f32),
        scratch_shapes=[pltpu.VMEM((total, width), bf16)] * 3 + [pltpu.VMEM(spread.shape, bf16)],
        compiler_params=SMALL,
        name="loss_blocks",
    )(slot, spread, *edges, *halos, w_prop, received, partner, mask)


def shifted(value, axis):
    devices = lax.axis_size(axis)
    up = [(i, i + 1) for i in range(devices - 1)]
    return lax.ppermute(value[0], axis, up), lax.ppermute(value[1], axis, [(j, i) for i, j in up])


def per_device(feat_query, feat_key, w_hidden, w_out, w_prop, valid_mask, neg_shard, neg_block):
    height, columns, _ = feat_query.shape
    pixels = height * columns
    per_tile = pixels // 128
    shards = lax.axis_size("rows")
    cols = lax.axis_size("cols")
    want, slot = plan_slots(neg_shard, neg_block, shards)
    req = lax.all_to_all(want, "rows", 0, 0, tiled=True)
    key_map = project(feat_key, w_hidden, w_out)
    width = key_map.shape[-1]
    partner = lax.ppermute(key_map, "cols", [(i, cols - 1 - i) for i in range(cols)])
    send = pack(req, key_map.reshape(per_tile, 128, width))
    received = lax.all_to_all(send, "rows", 0, 0, tiled=True)
    received = received.reshape(shards * CAP, 128, width)
    feat_query, _ = lax.optimization_barrier((feat_query, send))
    query, *edges = project(feat_query, w_hidden, w_out, True)
    first_row, last_row, first_col, last_col = edges
    top, bottom = shifted((last_row, first_row), "rows")
    first = jnp.concatenate([top[:1], first_col, bottom[:1]])
    last = jnp.concatenate([top[-1:], last_col, bottom[-1:]])
    left, right = shifted((last, first), "cols")
    halos = (top, bottom, left, right)
    spread = propagate(query, w_prop, columns)
    return loss_of(slot, spread, edges, halos, w_prop, received, partner, valid_mask)


def solution(mesh):
    in_specs = (
        P("rows", "cols", None),
        P("rows", "cols", None),
        P(),
        P(),
        P(),
        P("rows", "cols"),
        P("rows", "cols", None, None),
        P("rows", "cols", None, None),
    )
    out_specs = P("rows", "cols")
    return jax.shard_map(
        per_device, mesh=mesh, in_specs=in_specs, out_specs=out_specs, check_vma=False
    )
```
